128 devices in a mesh: rows: 8 (over y_lo, z), cols: 16 (over y_hi, x, core).
Axes of the slice: x: 4, y: 4 (y_hi: 2, y_lo: 2; y = y_hi * 2 + y_lo), z: 4, core: 2. Of those that a mesh axis runs over, the one named last changes fastest.
Arguments:
- frames: bfloat16 [4, 2048, 2048], P(None, 'rows', 'cols'), may hold values from -6 to 6
- enc_taps: float32 [9, 32], replicated, may hold values from -2 to 2
- enc_bias: float32 [32], replicated, may hold values from -3 to 3
- enc_proj: bfloat16 [512, 32], replicated, may hold values from -0.25 to 0.25
- w_in: bfloat16 [128, 512], replicated, may hold values from -0.5 to 0.5
- b_in: float32 [512], replicated, may hold values from -3 to 3
- ln_gain: float32 [512], replicated, may hold values from 0.1 to 1.9
- ln_bias: float32 [512], replicated, may hold values from -3 to 3
- spec_w1: float32 [2, 8, 64, 64], replicated, may hold values from -0.5 to 0.5
- spec_b1: float32 [2, 512], replicated, may hold values from -3 to 3
- spec_w2: float32 [2, 8, 64, 64], replicated, may hold values from -0.5 to 0.5
- spec_b2: float32 [2, 512], replicated, may hold values from -3 to 3
- cotangent: bfloat16 [512, 512, 512], P(('rows', 'cols')), may hold values from -6 to 6
Outputs:
- denoised: bfloat16 [512, 512, 512], P(('rows', 'cols'))
- grad_w_in: float32 [128, 512], replicated
- grad_b_in: float32 [512], replicated
- grad_ln_gain: float32 [512], replicated
- grad_ln_bias: float32 [512], replicated
- grad_w1: float32 [2, 8, 64, 64], replicated
- grad_b1: float32 [2, 512], replicated
- grad_w2: float32 [2, 8, 64, 64], replicated
- grad_b2: float32 [2, 512], replicated
The draws below stay inside these ranges and needn't reach their ends.
All inputs are finite; a program needn't handle non-finite values.
Results may differ from the reference program's by a relative error of at most 0.0039.
The reference program's roundings to bfloat16 on the way count: a program that leaves them out, or rounds other values in their place, can miss the bound.
Values may be sent and summed in bfloat16 or wider, within the bound.
A program may use at most 128 MiB of HBM per device.

```python
import math
import jax
import jax.numpy as jnp
from jax import lax

GRID = 2048
LAT = 512
FRAMES = 4
ENC_CH = 32
LAT_CH = 32
WIDTH = 512
BLOCKS = 8
KH = 128
KW_DEV = 1
N_ROWS = 8
N_COLS = 16


def steps_of(own_key, extent, pieces, low, largest):
    gain = 1.0
    for axis_at, shards_of in pieces:
        steps = jax.random.uniform(jax.random.fold_in(jax.random.fold_in(own_key, 6), axis_at), (shards_of,), jnp.float32, low / len(pieces), largest / len(pieces))
        gain = gain * jnp.repeat(jnp.exp(steps), extent[axis_at] // shards_of).reshape((-1,) + (1,) * (len(extent) - 1 - axis_at))
    return gain


def noise(rng, shape, scale, limit, pieces=(), kind=jnp.bfloat16):
    level = steps_of(rng, shape, pieces, -0.22, 0.18) if pieces else 1.0
    values = jax.random.normal(rng, shape, jnp.float32) * scale * level
    return jnp.minimum(jnp.maximum(values, -limit), limit).astype(kind)


def setup_inputs(seed: int = 0) -> dict:
    arg_keys = jax.random.split(jax.random.key(seed), 14)
    frames = noise(arg_keys[0], (FRAMES, GRID, GRID), 1.0, 6.0, ((1, 8), (2, 16)))
    enc_taps = noise(arg_keys[1], (9, ENC_CH), 9 ** -0.5, 2.0, (), jnp.float32)
    enc_bias = noise(arg_keys[2], (ENC_CH,), 0.5, 3.0, (), jnp.float32)
    enc_proj = noise(arg_keys[3], (ENC_CH * 16, LAT_CH), (ENC_CH * 16) ** -0.5, 0.25)
    w_in = noise(arg_keys[4], (FRAMES * LAT_CH, WIDTH), (FRAMES * LAT_CH) ** -0.5, 0.5)
    b_in = noise(arg_keys[5], (WIDTH,), 0.5, 3.0, (), jnp.float32)
    ln_gain = jnp.clip(1.0 + 0.18 * jax.random.normal(arg_keys[6], (WIDTH,), jnp.float32), 0.1, 1.9)
    ln_bias = noise(arg_keys[7], (WIDTH,), 0.5, 3.0, (), jnp.float32)
    spec_w1 = noise(arg_keys[8], (2, BLOCKS, WIDTH // BLOCKS, WIDTH // BLOCKS), (2 * (WIDTH // BLOCKS)) ** -0.5, 0.5, (), jnp.float32)
    spec_b1 = noise(arg_keys[9], (2, WIDTH), 0.5, 3.0, (), jnp.float32)
    spec_w2 = noise(arg_keys[10], (2, BLOCKS, WIDTH // BLOCKS, WIDTH // BLOCKS), (2 * (WIDTH // BLOCKS)) ** -0.5, 0.5, (), jnp.float32)
    spec_b2 = noise(arg_keys[11], (2, WIDTH), 0.5, 3.0, (), jnp.float32)
    cotangent = noise(arg_keys[12], (LAT, LAT, WIDTH), 1.0, 6.0, ((0, 128),))
    return {"frames": frames, "enc_taps": enc_taps, "enc_bias": enc_bias, "enc_proj": enc_proj, "w_in": w_in, "b_in": b_in, "ln_gain": ln_gain, "ln_bias": ln_bias, "spec_w1": spec_w1, "spec_b1": spec_b1, "spec_w2": spec_w2, "spec_b2": spec_b2, "cotangent": cotangent}


epsilon = 1e-05
highest = lax.Precision.HIGHEST

def width_tables(frequency, count):
    cell_index = jnp.arange(count, dtype=jnp.int32)
    angles = 2.0 * math.pi / count * jnp.mod(frequency[:, None] * cell_index[None, :], count).astype(jnp.float32)
    forward = jnp.stack([jnp.cos(angles), -jnp.sin(angles)])
    weights = jnp.where(frequency == 0, 1.0, 2.0).astype(jnp.float32)
    return (forward.astype(jnp.bfloat16), (forward * weights[None, :, None]).astype(jnp.bfloat16))

def height_table(cell_index, modes, count):
    frequency = jnp.arange(modes, dtype=jnp.int32) - modes // 2
    angles = 2.0 * math.pi / count * jnp.mod(frequency[:, None] * cell_index[None, :], count).astype(jnp.float32)
    cosine = jnp.cos(angles)
    sine_table = jnp.sin(angles)
    first = jnp.stack([cosine, sine_table], axis=-1)
    second = jnp.stack([-sine_table, cosine], axis=-1)
    return jnp.concatenate([first, second], axis=0).astype(jnp.bfloat16)

def mixed(form, left, right):
    return jnp.einsum(form, left.astype(jnp.float32), right.astype(jnp.float32), precision=highest)

def conv_project(padded, enc_taps, enc_bias, patch_proj):
    height = padded.shape[0] - 2
    breadth = padded.shape[1] - 2
    values = padded.astype(jnp.float32)
    hidden = jnp.broadcast_to(enc_bias[:, None, None], (enc_taps.shape[1], height, breadth))
    for tap_index in range(9):
        offset_down = tap_index // 3
        offset_side = tap_index % 3
        hidden = hidden + enc_taps[tap_index][:, None, None] * values[None, offset_down:offset_down + height, offset_side:offset_side + breadth]
    hidden = jnp.maximum(hidden, 0.0).astype(jnp.bfloat16)
    blocks = hidden.reshape(hidden.shape[0], height // 4, 4, breadth // 4, 4)
    return mixed('caybx,cyxo->abo', blocks, patch_proj)

def embed(latent, w_in, b_in, ln_gain, ln_bias):
    flat = latent.reshape(-1, latent.shape[-1])
    embedded = (jnp.dot(flat.astype(jnp.float32), w_in.astype(jnp.float32), precision=highest) + b_in).reshape(latent.shape[0], latent.shape[1], -1)
    average = lax.optimization_barrier(jnp.mean(embedded, axis=-1, keepdims=True))
    centered = embedded - average
    inverse_std = lax.rsqrt(lax.optimization_barrier(jnp.mean(centered * centered, axis=-1, keepdims=True)) + epsilon)
    normalized = centered * inverse_std
    normed = (normalized * ln_gain + ln_bias).astype(jnp.bfloat16)
    return (embedded, normalized, inverse_std, normed)

def complex_block(real_part, imag_part, weight):

    def times_block(values, matrix):
        return jnp.einsum('mbi,bio->mbo', values, matrix, precision=highest)
    return (times_block(real_part, weight[0]) - times_block(imag_part, weight[1]), times_block(real_part, weight[1]) + times_block(imag_part, weight[0]))

def complex_back(real_part, imag_part, grad_real, grad_imag, weight):

    def transposed(values, matrix):
        return jnp.einsum('mbo,bio->mbi', values, matrix, precision=highest)

    def outer_sum(left, right):
        return jnp.einsum('mbi,mbo->bio', left, right, precision=highest)
    in_real = transposed(grad_real, weight[0]) + transposed(grad_imag, weight[1])
    in_imag = transposed(grad_imag, weight[0]) - transposed(grad_real, weight[1])
    grad_weight = jnp.stack([outer_sum(real_part, grad_real) + outer_sum(imag_part, grad_imag), outer_sum(real_part, grad_imag) - outer_sum(imag_part, grad_real)])
    return (in_real, in_imag, grad_weight)

def spectral_forward(coeffs, spec_w1, spec_b1, spec_w2, spec_b2):
    blocks = spec_w1.shape[1]
    block_size = spec_w1.shape[2]
    real_part = coeffs[0].reshape(-1, blocks, block_size)
    imag_part = coeffs[1].reshape(-1, blocks, block_size)
    pre_real, pre_imag = complex_block(real_part, imag_part, spec_w1)
    pre_real = pre_real + spec_b1[0].reshape(blocks, block_size)
    pre_imag = pre_imag + spec_b1[1].reshape(blocks, block_size)
    act_real = jax.nn.gelu(pre_real)
    act_imag = jax.nn.gelu(pre_imag)
    out_real, out_imag = complex_block(act_real, act_imag, spec_w2)
    out_real = out_real + spec_b2[0].reshape(blocks, block_size)
    out_imag = out_imag + spec_b2[1].reshape(blocks, block_size)
    mixed_modes = jnp.stack([out_real, out_imag]).reshape(coeffs.shape)
    return (mixed_modes, (real_part, imag_part, pre_real, pre_imag, act_real, act_imag))

def spectral_backward(stored, grad_modes, spec_w1, spec_w2):
    real_part, imag_part, pre_real, pre_imag, act_real, act_imag = stored
    blocks = spec_w1.shape[1]
    block_size = spec_w1.shape[2]
    grad_real = grad_modes[0].reshape(-1, blocks, block_size)
    grad_imag = grad_modes[1].reshape(-1, blocks, block_size)
    grad_b2 = jnp.stack([lax.optimization_barrier(jnp.sum(grad_real, axis=0)).reshape(-1), lax.optimization_barrier(jnp.sum(grad_imag, axis=0)).reshape(-1)])
    back_real, back_imag, grad_w2 = complex_back(act_real, act_imag, grad_real, grad_imag, spec_w2)
    back_real = jax.vjp(jax.nn.gelu, pre_real)[1](back_real)[0]
    back_imag = jax.vjp(jax.nn.gelu, pre_imag)[1](back_imag)[0]
    grad_b1 = jnp.stack([lax.optimization_barrier(jnp.sum(back_real, axis=0)).reshape(-1), lax.optimization_barrier(jnp.sum(back_imag, axis=0)).reshape(-1)])
    in_real, in_imag, grad_w1 = complex_back(real_part, imag_part, back_real, back_imag, spec_w1)
    grad_coeffs = jnp.stack([in_real, in_imag]).reshape(grad_modes.shape)
    return (grad_coeffs, grad_w1, grad_b1, grad_w2, grad_b2)

def reference(frames, enc_taps, enc_bias, enc_proj, w_in, b_in, ln_gain, ln_bias, spec_w1, spec_b1, spec_w2, spec_b2, cotangent):
    side = GRID // 4
    factor = side ** (-0.5)
    channels = FRAMES * LAT_CH
    padded = jnp.pad(frames, ((0, 0), (1, 1), (1, 1)))
    patch_proj = enc_proj.reshape(ENC_CH, 4, 4, LAT_CH)
    strip_rows = GRID // 16

    def encode_strip(strip_index):
        start = (strip_index * strip_rows).astype(jnp.int32)
        piece = lax.dynamic_slice_in_dim(padded, start, strip_rows + 2, 1)
        parts = [conv_project(piece[frame_index], enc_taps, enc_bias, patch_proj) for frame_index in range(FRAMES)]
        return jnp.concatenate(parts, axis=-1).astype(jnp.bfloat16)
    latent = lax.map(encode_strip, jnp.arange(16, dtype=jnp.int32)).reshape(side, side, channels)
    modes = KW_DEV * N_ROWS * N_COLS
    wave_fwd, wave_inv = width_tables(jnp.arange(modes, dtype=jnp.int32), side)
    rotation = height_table(jnp.arange(side, dtype=jnp.int32), KH, side)
    block_rows = side // 16
    block_starts = jnp.arange(16, dtype=jnp.int32) * block_rows

    def rows_of(array, start):
        return lax.dynamic_slice_in_dim(array, start.astype(jnp.int32), block_rows, 0)

    def to_spectrum(start):
        normed = embed(rows_of(latent, start), w_in, b_in, ln_gain, ln_bias)[3]
        return (mixed('pkn,hnc->hpkc', wave_fwd, normed) * factor).astype(jnp.bfloat16)
    spectrum = lax.map(to_spectrum, block_starts).reshape(side, 2, modes, WIDTH)
    coeffs = (mixed('qhp,hpkc->qkc', rotation, spectrum) * factor).reshape(2, KH, modes, WIDTH)
    mixed_modes, stored = spectral_forward(coeffs, spec_w1, spec_b1, spec_w2, spec_b2)
    modes_bf = mixed_modes.astype(jnp.bfloat16).reshape(2 * KH, modes, WIDTH)
    grid_back = (mixed('qhp,qkc->hpkc', rotation, modes_bf) * factor).astype(jnp.bfloat16)

    def to_output(start):
        embedded = embed(rows_of(latent, start), w_in, b_in, ln_gain, ln_bias)[0]
        branch = mixed('pkn,hpkc->hnc', wave_inv, rows_of(grid_back, start)) * factor
        return (embedded + branch).astype(jnp.bfloat16)
    denoised = lax.map(to_output, block_starts).reshape(side, side, WIDTH)

    def to_grad_grid(start):
        return (mixed('pkn,hnc->hpkc', wave_inv, rows_of(cotangent, start)) * factor).astype(jnp.bfloat16)
    grad_grid = lax.map(to_grad_grid, block_starts).reshape(side, 2, modes, WIDTH)
    grad_modes = (mixed('qhp,hpkc->qkc', rotation, grad_grid) * factor).reshape(2, KH, modes, WIDTH)
    grad_coeffs, grad_w1, grad_b1, grad_w2, grad_b2 = spectral_backward(stored, grad_modes, spec_w1, spec_w2)
    coeffs_bf = grad_coeffs.astype(jnp.bfloat16).reshape(2 * KH, modes, WIDTH)
    grad_cells = (mixed('qhp,qkc->hpkc', rotation, coeffs_bf) * factor).astype(jnp.bfloat16)

    def token_step(carry, start):
        latent_rows = rows_of(latent, start)
        embedded, normalized, inverse_std, normed = embed(latent_rows, w_in, b_in, ln_gain, ln_bias)
        grad_normed = mixed('pkn,hpkc->hnc', wave_fwd, rows_of(grad_cells, start)) * factor
        scaled = grad_normed * ln_gain
        grad_embedded = rows_of(cotangent, start).astype(jnp.float32) + inverse_std * (scaled - lax.optimization_barrier(jnp.mean(scaled, axis=-1, keepdims=True)) - normalized * lax.optimization_barrier(jnp.mean(scaled * normalized, axis=-1, keepdims=True)))
        grad_bf = grad_embedded.astype(jnp.bfloat16)
        terms = (mixed('hni,hnc->ic', latent_rows, grad_bf), lax.optimization_barrier(jnp.sum(grad_embedded, axis=(0, 1))), lax.optimization_barrier(jnp.sum(grad_normed * normalized, axis=(0, 1))), lax.optimization_barrier(jnp.sum(grad_normed, axis=(0, 1))))
        return (tuple((total + term for total, term in zip(carry, terms))), None)
    zeros = (jnp.zeros((channels, WIDTH), jnp.float32), jnp.zeros((WIDTH,), jnp.float32), jnp.zeros((WIDTH,), jnp.float32), jnp.zeros((WIDTH,), jnp.float32))
    totals = lax.scan(token_step, zeros, block_starts)[0]
    grad_w_in, grad_b_in, grad_ln_gain, grad_ln_bias = totals
    return (denoised, grad_w_in, grad_b_in, grad_ln_gain, grad_ln_bias, grad_w1, grad_b1, grad_w2, grad_b2)
```

```python
import functools
import math

import jax
import jax.numpy as jnp
import ml_dtypes
import numpy as np
from jax import lax
from jax.experimental import pallas as pl
from jax.experimental.pallas import tpu as pltpu
from jax.sharding import PartitionSpec as P

F32 = jnp.float32
BF16 = jnp.bfloat16
MESH = pl.DeviceIdType.MESH
HIGHEST = lax.Precision.HIGHEST

NR, NC = 8, 16
ND = NR * NC
LAT = 512
WIDTH = 512
KH = 128
ROWS = 4
FRAMES = 4
STEP = 37
EPS = 1e-05
FACTOR = LAT ** (-0.5)
CUBE = 0.044715
ROOT = math.sqrt(2.0 / math.pi)


def tables():
    n = np.arange(LAT)
    k = np.arange(ND)
    angle = ((k[:, None] * n[None, :]) % LAT).astype(np.float32) * np.float32(2.0 * math.pi / LAT)
    fwd = np.stack([np.cos(angle.astype(np.float64)), -np.sin(angle.astype(np.float64))]).astype(np.float32)
    inv = fwd * np.where(k == 0, 1.0, 2.0).astype(np.float32)[None, :, None]
    order = lambda t: t.reshape(2, 32, 4, LAT).transpose(2, 0, 1, 3).reshape(256, LAT).astype(ml_dtypes.bfloat16)
    m = np.arange(KH) - KH // 2
    u = (np.mod(m[:, None] * n[None, :], LAT)).astype(np.float32) * np.float32(2.0 * math.pi / LAT)
    cos, sin = np.cos(u.astype(np.float64)), np.sin(u.astype(np.float64))
    rot = np.concatenate([np.stack([cos, sin], -1), np.stack([-sin, cos], -1)], 0)
    rot = rot.astype(np.float32).reshape(2 * KH, 2 * LAT).astype(ml_dtypes.bfloat16)
    wf, wi = order(fwd), order(inv)
    place = np.zeros((16, 48, 144), np.float32)
    for y in range(4):
        for x in range(4):
            for part in range(3):
                for tap in range(9):
                    place[4 * y + x, 16 * part + tap, 48 * part + 8 * (y + tap // 3) + x + tap % 3] = 1.0
                place[4 * y + x, 16 * part + 9, 48 * part + 6] = 1.0
    return wf, wi, np.ascontiguousarray(wf.T), np.ascontiguousarray(wi.T), rot, np.ascontiguousarray(rot.T), place.astype(ml_dtypes.bfloat16)


def dot(a, b, precision=None):
    return jnp.dot(a, b, preferred_element_type=F32, precision=precision)


def dot_t(a, b, dims, precision=None):
    return lax.dot_general(a, b, (dims, ((), ())), preferred_element_type=F32, precision=precision)


def gelu_pair(v):
    squared = v * v
    t = jnp.tanh(ROOT * (v + CUBE * (squared * v)))
    half = 0.5 * (1.0 + t)
    slope = half + 0.5 * v * (1.0 - t * t) * (ROOT * (1.0 + (3.0 * CUBE) * squared))
    return v * half, slope


def kernel(
    frames, taps, bias, proj, w_in, b_in, gain, lbias, w1, b1, w2, b2, cot_hbm,
    wf, wi, wft, wit, rot, rott, place,
    den_hbm, gwin, gbin, ggain, gbias, gw1, gb1, gw2, gb2,
    cot, ft, fsend, htop, hbot, frecv, rtop, rbot, est, wbig, projt, tp, lat, emb, nrm, istd, den,
    stage, snd, rcv, wc1, wc2, bc, wsend, wrecv, agw, fsnd, frcv, agf,
    lsem, fss, frs, hss, hrs, ass, ars, als, wss, wrs, gss, grs, rss, rrs, qss, qrs,
):
    r = lax.axis_index("rows")
    c = lax.axis_index("cols")
    me = r * NC + c
    kg = me // 4
    cg = lax.rem(me, 4)

    def coord(d):
        return (d // NC, lax.rem(d, NC))

    def peer(i):
        return lax.rem(me + lax.rem(i * STEP, ND), ND)

    cot_in = pltpu.make_async_copy(cot_hbm, cot, lsem.at[0])
    cot_in.start()
    barrier = pltpu.get_barrier_semaphore()

    @pl.loop(1, ND)
    def _(i):
        pl.semaphore_signal(barrier, inc=1, device_id=coord(peer(i)), device_id_type=MESH)

    zero8 = jnp.zeros((8, 128), F32)
    for f in range(FRAMES):
        ft[f, 0:8, :] = zero8
        ft[f, 264:272, :] = zero8
        ft[f, 8:264, :] = frames[f].astype(F32)
    for f in range(FRAMES):
        for j in range(NC):
            fsend[j, f] = ft[f, 16 * j + 7 : 16 * j + 31, :].reshape(3, 8, 128).astype(BF16)
        htop[f] = ft[f, 263:271, :].astype(BF16)
        hbot[f] = ft[f, 7:15, :].astype(BF16)
    pl.semaphore_wait(barrier, ND - 1)

    def frame_copy(i):
        j = lax.rem(c + i, NC)
        return pltpu.make_async_remote_copy(
            fsend.at[j], frecv.at[c], fss, frs, device_id=(r, j), device_id_type=MESH)

    @pl.loop(1, NC)
    def _(i):
        frame_copy(i).start()

    own_frames = pltpu.make_async_copy(fsend.at[c], frecv.at[c], lsem.at[1])
    own_frames.start()

    @pl.when(r < NR - 1)
    def _():
        pltpu.make_async_remote_copy(
            htop, rtop.at[c], hss.at[0], hrs.at[0], device_id=(r + 1, 0), device_id_type=MESH).start()

    @pl.when(r > 0)
    def _():
        pltpu.make_async_remote_copy(
            hbot, rbot.at[c], hss.at[1], hrs.at[1], device_id=(r - 1, NC - 1), device_id_type=MESH).start()

    has_top = jnp.logical_and(c == 0, r > 0)
    has_bot = jnp.logical_and(c == NC - 1, r < NR - 1)

    @pl.when(jnp.logical_not(has_top))
    def _():
        rtop[...] = jnp.zeros(rtop.shape, BF16)

    @pl.when(jnp.logical_not(has_bot))
    def _():
        rbot[...] = jnp.zeros(rbot.shape, BF16)

    def send_all(e):
        pltpu.make_async_copy(snd.at[e, me], rcv.at[e, me], als.at[e]).start()

        @pl.loop(1, ND)
        def _(i):
            d = peer(i)
            pltpu.make_async_remote_copy(
                snd.at[e, d], rcv.at[e, me], ass.at[e], ars.at[e], device_id=coord(d), device_id_type=MESH).start()

    def all_but_one(buf, ss, rs, count):
        part = buf.at[pl.ds(0, count)]
        return pltpu.make_async_remote_copy(part, part, ss, rs, device_id=coord(peer(1)), device_id_type=MESH)

    def recv_all(e):
        pltpu.make_async_copy(snd.at[e, me], rcv.at[e, me], als.at[e]).wait()
        all_but_one(rcv.at[e], ass.at[e], ars.at[e], ND - 1).wait_recv()

    def put_rows(h, value):
        for k4 in range(4):
            for p in range(2):
                rows = value[k4 * 64 + p * 32 : k4 * 64 + p * 32 + 32, :]
                for g in range(4):
                    stage[k4, pl.ds(8 * g + 2 * h + p, 32, stride=32), :] = rows[:, 128 * g : 128 * g + 128]

    def pack(e):
        for k4 in range(4):
            snd[e, :, :, 128 * k4 : 128 * k4 + 128] = stage[k4].reshape(ND, 8, 128).astype(BF16)

    cot_in.wait()
    for h in range(ROWS):
        put_rows(h, dot(wi[...], cot[h]) * FACTOR)
    pack(0)
    send_all(0)

    tp[...] = jnp.zeros(tp.shape, F32)
    tp[0:9, :] = taps[...]
    tp[9:10, :] = bias[...]
    whole = tp[...]
    high = whole.astype(BF16)
    rest = whole - high.astype(F32)
    mid = rest.astype(BF16)
    low = (rest - mid.astype(F32)).astype(BF16)
    parts = jnp.concatenate([high, mid, low], axis=0)
    for yx in range(16):
        wbig[32 * yx : 32 * yx + 32, :] = dot_t(parts, place[yx], ((0,), (0,))).astype(BF16)
    row = lax.broadcasted_iota(jnp.int32, (512, 512), 0)
    col = lax.broadcasted_iota(jnp.int32, (512, 512), 1)
    to_yxc = (row == (col & 31) * 16 + (col >> 5)).astype(F32).astype(BF16)
    projt[...] = dot_t(proj[...], to_yxc, ((0,), (0,))).astype(BF16)
    to_phase = (row == (col & 127) * 4 + (col >> 7)).astype(F32).astype(BF16)
    for wc, w in ((wc1, w1), (wc2, w2)):
        wc[...] = jnp.zeros(wc.shape, F32)
        for b in range(2):
            real = w[0, 2 * cg + b]
            imag = w[1, 2 * cg + b]
            lo, hi = 64 * b, 64 * b + 64
            wc[lo:hi, lo:hi] = real
            wc[128 + lo : 128 + hi, 128 + lo : 128 + hi] = real
            wc[lo:hi, 128 + lo : 128 + hi] = imag
            wc[128 + lo : 128 + hi, lo:hi] = -imag
    lanes = pl.ds(pl.multiple_of(cg * 128, 128), 128)
    bias1 = jnp.concatenate([b1[0:1, lanes], b1[1:2, lanes]], axis=1)
    bias2 = jnp.concatenate([b2[0:1, lanes], b2[1:2, lanes]], axis=1)
    for f in range(FRAMES):
        for t in range(4):
            est[f, t, pl.ds(6, 24, stride=8), :] = jnp.ones((24, 128), F32)
            est[f, t, pl.ds(7, 24, stride=8), :] = jnp.zeros((24, 128), F32)

    own_frames.wait()
    all_but_one(frecv, fss, frs, NC - 1).wait_recv()

    @pl.when(has_top)
    def _():
        pltpu.make_async_remote_copy(rtop, rtop, hss.at[0], hrs.at[0], device_id=(r, c), device_id_type=MESH).wait_recv()

    @pl.when(has_bot)
    def _():
        pltpu.make_async_remote_copy(rbot, rbot, hss.at[1], hrs.at[1], device_id=(r, c), device_id_type=MESH).wait_recv()

    split = []
    for g in range(4):
        pieces = []
        for j in range(4):
            v = frecv[4 * g + j].astype(F32)
            up = v[:, 0] + rtop[4 * g + j].astype(F32)
            down = v[:, 2] + rbot[4 * g + j].astype(F32)
            pieces.append(jnp.stack([up, v[:, 1], down], axis=1).reshape(96, 128).astype(BF16))
        split.append(dot(jnp.concatenate(pieces, axis=1), to_phase))
    lane = lax.broadcasted_iota(jnp.int32, (96, 512), 1)
    first = jnp.concatenate([s[:, 0:128] for s in split], axis=1)
    last = jnp.concatenate([s[:, 384:512] for s in split], axis=1)
    before = jnp.where(lane == 0, 0.0, pltpu.roll(last, 1, axis=1))
    after = jnp.where(lane == LAT - 1, 0.0, pltpu.roll(first, LAT - 1, axis=1))
    for t in range(4):
        own = slice(128 * t, 128 * t + 128)
        planes = [before[:, own]] + [split[t][:, 128 * q : 128 * q + 128] for q in range(4)] + [after[:, own]]
        for x, plane in enumerate(planes):
            for f in range(FRAMES):
                est[f, t, pl.ds(x, 24, stride=8), :] = plane[24 * f : 24 * f + 24, :]

    @pl.loop(0, ROWS)
    def _(h):
        for f in range(FRAMES):
            top = pl.multiple_of(32 * h, 32)
            patch = jnp.concatenate([est[f, t, pl.ds(top, 48), :] for t in range(4)], axis=1).astype(BF16)
            hidden = dot(wbig[...], jnp.concatenate([patch, patch, patch], axis=0))
            hidden = jnp.maximum(hidden, 0.0).astype(BF16)
            lat[h, 32 * f : 32 * f + 32, :] = dot(projt[...], hidden).astype(BF16)

    for h in range(ROWS):
        embedded = dot_t(lat[h], w_in[...], ((0,), (0,))) + b_in[...]
        emb[h] = embedded
        centered = embedded - jnp.mean(embedded, axis=1, keepdims=True)
        inverse = lax.rsqrt(jnp.mean(centered * centered, axis=1, keepdims=True) + EPS)
        normalized = centered * inverse
        istd[h] = inverse
        nrm[h] = normalized
        normed = (normalized * gain[...] + lbias[...]).astype(BF16)
        put_rows(h, dot(wf[...], normed) * FACTOR)
    pack(1)
    send_all(1)

    def to_modes(e):
        x = rcv[e].astype(F32).reshape(2 * LAT, 512).astype(BF16)
        return stacked(dot(rot[...], x) * FACTOR)

    def stacked(v):
        return jnp.concatenate(
            [jnp.concatenate([v[0:KH, 128 * q : 128 * q + 128], v[KH:, 128 * q : 128 * q + 128]], axis=1) for q in range(4)], axis=0)

    def unstacked(v):
        return jnp.concatenate(
            [jnp.concatenate([v[KH * q : KH * q + KH, 128 * p : 128 * p + 128] for q in range(4)], axis=1) for p in range(2)], axis=0)

    def from_modes(e, v):
        back = dot(rott[...], unstacked(v).astype(BF16)) * FACTOR
        snd[e] = back.reshape(ND, 8, 512).astype(BF16)
        send_all(e)

    recv_all(0)
    grad = to_modes(0)
    recv_all(1)
    coeffs = to_modes(1)
    pre = dot(coeffs, wc1[...], HIGHEST) + bias1
    act, slope = gelu_pair(pre)
    from_modes(2, dot(act, wc2[...], HIGHEST) + bias2)
    back = dot_t(grad, wc2[...], ((1,), (1,)), HIGHEST) * slope
    from_modes(3, dot_t(back, wc1[...], ((1,), (1,)), HIGHEST))

    half = lax.broadcasted_iota(jnp.int32, (64, 128), 1) < 64

    def weight_grad(left, right):
        g = dot_t(left, right, ((0,), (0,)), HIGHEST)
        real = g[0:128, 0:128] + g[128:256, 128:256]
        imag = g[0:128, 128:256] - g[128:256, 0:128]
        return [jnp.where(half, v[0:64, :], v[64:128, :]) for v in (real, imag)]

    tiles = weight_grad(coeffs, back) + weight_grad(act, grad)
    wsend[...] = jnp.concatenate(tiles, axis=0).reshape(32, 8, 128)
    wrecv[kg] = wsend[kg]

    @pl.loop(1, 32)
    def _(i):
        j = lax.rem(kg + i, 32)
        pltpu.make_async_remote_copy(
            wsend.at[j], wrecv.at[kg], wss, wrs, device_id=coord(4 * j + cg), device_id_type=MESH).start()

    sum1 = jnp.sum(back, axis=0, keepdims=True)
    sum2 = jnp.sum(grad, axis=0, keepdims=True)
    bc[...] = jnp.zeros(bc.shape, F32)
    for p in range(2):
        bc[p : p + 1, lanes] = sum1[:, 128 * p : 128 * p + 128]
        bc[2 + p : 3 + p, lanes] = sum2[:, 128 * p : 128 * p + 128]

    def get_rows(e, h):
        blocks = []
        for k4 in range(4):
            for q in range(2):
                blocks.append(jnp.concatenate(
                    [stage[k4, pl.ds(8 * g + 2 * h + q, 32, stride=32), :] for g in range(4)], axis=1))
        return jnp.concatenate(blocks, axis=0).astype(BF16)

    def unpack(e):
        for k4 in range(4):
            stage[k4] = rcv[e, :, :, 128 * k4 : 128 * k4 + 128].astype(F32).reshape(8 * ND, 128)

    recv_all(2)
    unpack(2)
    for h in range(ROWS):
        den[h] = (emb[h] + dot(wit[...], get_rows(2, h)) * FACTOR).astype(BF16)
        pltpu.make_async_copy(den.at[h], den_hbm.at[h], lsem.at[2 + h]).start()

    all_but_one(wrecv, wss, wrs, 31).wait_recv()
    total = wrecv[0]
    for j in range(1, 32):
        total = total + wrecv[j]
    agw[kg, cg] = total

    @pl.loop(1, ND)
    def _(i):
        pltpu.make_async_remote_copy(
            agw.at[kg, cg], agw.at[kg, cg], gss, grs, device_id=coord(peer(i)), device_id_type=MESH).start()

    recv_all(3)
    unpack(3)
    sums = [jnp.zeros((1, WIDTH), F32) for _ in range(3)]
    weight = jnp.zeros((128, WIDTH), F32)
    for h in range(ROWS):
        gn = dot(wft[...], get_rows(3, h)) * FACTOR
        normalized = nrm[h]
        sums[1] = sums[1] + jnp.sum(gn * normalized, axis=0, keepdims=True)
        sums[2] = sums[2] + jnp.sum(gn, axis=0, keepdims=True)
        scaled = gn * gain[...]
        ge = cot[h].astype(F32) + istd[h] * (
            scaled
            - jnp.mean(scaled, axis=1, keepdims=True)
            - normalized * jnp.mean(scaled * normalized, axis=1, keepdims=True))
        sums[0] = sums[0] + jnp.sum(ge, axis=0, keepdims=True)
        weight = weight + dot(lat[h], ge.astype(BF16))

    for b in range(4):
        own = slice(128 * b, 128 * b + 128)
        for a in range(32):
            fsnd[4 * a + b, 0:4, :] = weight[4 * a : 4 * a + 4, own]
        for a in range(3):
            fsnd[4 * a + b, 4:5, :] = sums[a][:, own]
        for a in range(4):
            fsnd[4 * (a + 3) + b, 4:5, :] = bc[a : a + 1, own]
        for a in range(7, 32):
            fsnd[4 * a + b, 4:5, :] = jnp.zeros((1, 128), F32)
    for d in range(ND):
        fsnd[d, 5:8, :] = jnp.zeros((3, 128), F32)
    frcv[me] = fsnd[me]

    @pl.loop(1, ND)
    def _(i):
        d = peer(i)
        pltpu.make_async_remote_copy(
            fsnd.at[d], frcv.at[me], rss, rrs, device_id=coord(d), device_id_type=MESH).start()

    all_but_one(frcv, rss, rrs, ND - 1).wait_recv()
    agf[me] = jnp.sum(frcv[...], axis=0)

    @pl.loop(1, ND)
    def _(i):
        pltpu.make_async_remote_copy(
            agf.at[me], agf.at[me], qss, qrs, device_id=coord(peer(i)), device_id_type=MESH).start()

    everyone = dict(device_id=coord(peer(1)), device_id_type=MESH)
    agw_most = pltpu.make_async_remote_copy(frcv.at[pl.ds(0, ND - 1)], frcv.at[pl.ds(0, ND - 1)], gss, grs, **everyone)
    agw_most.wait_recv()
    for w, (gw, gb) in enumerate(((gw1, gb1), (gw2, gb2))):
        for p in range(2):
            for g in range(4):
                v = agw[16 * w + 8 * p : 16 * w + 8 * p + 8, g].reshape(64, 128)
                gw[p, 2 * g] = v[:, 0:64]
                gw[p, 2 * g + 1] = v[:, 64:128]

    all_but_one(agf, qss, qrs, ND - 1).wait_recv()
    small = [gbin, ggain, gbias]
    for b in range(4):
        own = slice(128 * b, 128 * b + 128)
        for a in range(32):
            gwin[4 * a : 4 * a + 4, own] = agf[4 * a + b, 0:4, :]
        for a in range(3):
            small[a][:, own] = agf[4 * a + b, 4:5, :]
        for a in range(2):
            gb1[a : a + 1, own] = agf[4 * (a + 3) + b, 4:5, :]
            gb2[a : a + 1, own] = agf[4 * (a + 5) + b, 4:5, :]

    for h in range(ROWS):
        pltpu.make_async_copy(den.at[h], den_hbm.at[h], lsem.at[2 + h]).wait()
    all_but_one(frecv, fss, frs, NC - 1).wait_send()

    @pl.when(r < NR - 1)
    def _():
        pltpu.make_async_remote_copy(htop, htop, hss.at[0], hrs.at[0], device_id=(r, c), device_id_type=MESH).wait_send()

    @pl.when(r > 0)
    def _():
        pltpu.make_async_remote_copy(hbot, hbot, hss.at[1], hrs.at[1], device_id=(r, c), device_id_type=MESH).wait_send()

    for e in range(4):
        all_but_one(rcv.at[e], ass.at[e], ars.at[e], ND - 1).wait_send()
    all_but_one(wrecv, wss, wrs, 31).wait_send()
    agw_most.wait_send()
    all_but_one(frcv, rss, rrs, ND - 1).wait_send()
    all_but_one(agf, qss, qrs, ND - 1).wait_send()


def body(frames, enc_taps, enc_bias, enc_proj, w_in, b_in, ln_gain, ln_bias, spec_w1, spec_b1, spec_w2, spec_b2, cotangent):
    wf, wi, wft, wit, rot, rott, place = (jnp.asarray(t) for t in tables())
    vmem = pl.BlockSpec(memory_space=pltpu.VMEM)
    hbm = pl.BlockSpec(memory_space=pl.ANY)
    shape = jax.ShapeDtypeStruct
    dma = pltpu.SemaphoreType.DMA
    outs = pl.pallas_call(
        kernel,
        out_shape=(
            shape((ROWS, LAT, WIDTH), BF16), shape((128, WIDTH), F32), shape((1, WIDTH), F32), shape((1, WIDTH), F32),
            shape((1, WIDTH), F32), shape((2, 8, 64, 64), F32), shape((2, WIDTH), F32), shape((2, 8, 64, 64), F32),
            shape((2, WIDTH), F32)),
        in_specs=[vmem] * 12 + [hbm] + [vmem] * 7,
        out_specs=(hbm,) + (vmem,) * 8,
        scratch_shapes=[
            pltpu.VMEM((ROWS, LAT, WIDTH), BF16),
            pltpu.VMEM((FRAMES, 272, 128), F32),
            pltpu.VMEM((NC, FRAMES, 3, 8, 128), BF16),
            pltpu.VMEM((FRAMES, 8, 128), BF16),
            pltpu.VMEM((FRAMES, 8, 128), BF16),
            pltpu.VMEM((NC, FRAMES, 3, 8, 128), BF16),
            pltpu.VMEM((NC, FRAMES, 8, 128), BF16),
            pltpu.VMEM((NC, FRAMES, 8, 128), BF16),
            pltpu.VMEM((FRAMES, 4, 192, 128), F32),
            pltpu.VMEM((512, 144), BF16),
            pltpu.VMEM((32, 512), BF16),
            pltpu.VMEM((16, 32), F32),
            pltpu.VMEM((ROWS, 128, LAT), BF16),
            pltpu.VMEM((ROWS, LAT, WIDTH), F32),
            pltpu.VMEM((ROWS, LAT, WIDTH), F32),
            pltpu.VMEM((ROWS, LAT, 1), F32),
            pltpu.VMEM((ROWS, LAT, WIDTH), BF16),
            pltpu.VMEM((4, 8 * ND, 128), F32),
            pltpu.VMEM((4, ND, 8, 512), BF16),
            pltpu.VMEM((4, ND, 8, 512), BF16),
            pltpu.VMEM((256, 256), F32),
            pltpu.VMEM((256, 256), F32),
            pltpu.VMEM((8, WIDTH), F32),
            pltpu.VMEM((32, 8, 128), F32),
            pltpu.VMEM((32, 8, 128), F32),
            pltpu.VMEM((32, 4, 8, 128), F32),
            pltpu.VMEM((ND, 8, 128), F32),
            pltpu.VMEM((ND, 8, 128), F32),
            pltpu.VMEM((ND, 8, 128), F32),
            dma((8,)), dma(()), dma(()), dma((2,)), dma((2,)), dma((4,)), dma((4,)), dma((4,)),
            dma(()), dma(()), dma(()), dma(()), dma(()), dma(()), dma(()), dma(()),
        ],
        compiler_params=pltpu.CompilerParams(
            collective_id=0, has_side_effects=True, vmem_limit_bytes=64 * 1000 * 1000),
        name="step",
    )(
        frames, enc_taps, enc_bias.reshape(1, -1), enc_proj, w_in, b_in.reshape(1, -1), ln_gain.reshape(1, -1),
        ln_bias.reshape(1, -1), spec_w1, spec_b1, spec_w2, spec_b2, cotangent,
        wf, wi, wft, wit, rot, rott, place)
    den, gwin, gbin, ggain, gbias, gw1, gb1, gw2, gb2 = outs
    return (den, gwin, gbin.reshape(-1), ggain.reshape(-1), gbias.reshape(-1), gw1, gb1, gw2, gb2)


def solution(mesh):
    return jax.shard_map(
        body,
        mesh=mesh,
        in_specs=(P(None, "rows", "cols"),) + (P(),) * 11 + (P(("rows", "cols"), None, None),),
        out_specs=(P(("rows", "cols"), None, None),) + (P(),) * 8,
        check_vma=False,
    )
```

```python
import itertools
import math
import random

import jax
import jax.numpy as jnp
import ml_dtypes
import numpy as np
from jax import lax
from jax.experimental import pallas as pl
from jax.experimental.pallas import tpu as pltpu
from jax.sharding import PartitionSpec as P

F32 = jnp.float32
BF16 = jnp.bfloat16
HIGHEST = lax.Precision.HIGHEST

NR, NC = 8, 16
ND = NR * NC
LAT = 512
WIDTH = 512
KH = 128
ROWS = 4
FRAMES = 4


def far_first():
    offsets = [o for o in itertools.product(range(4), range(2), range(2), range(4), range(2)) if any(o)]
    random.Random(1).shuffle(offsets)
    y_hops = {(0, 0): 0, (1, 0): 1, (0, 1): 2, (1, 1): 1}
    return sorted(offsets, key=lambda o: -(min(o[0], 4 - o[0]) + min(o[3], 4 - o[3]) + y_hops[o[1], o[2]]))


PEERS = far_first()
COT_FIRST = 48
OUT_FIRST = 80
VMEM_LIMIT = 44 * 1024 * 1024
EPS = 1e-05
FACTOR = LAT ** (-0.5)
CUBE = 0.044715
ROOT = math.sqrt(2.0 / math.pi)


def tables():
    n = np.arange(LAT)
    k = np.arange(ND)
    angle = ((k[:, None] * n[None, :]) % LAT).astype(np.float32) * np.float32(2.0 * math.pi / LAT)
    fwd = np.stack([np.cos(angle.astype(np.float64)), -np.sin(angle.astype(np.float64))]).astype(np.float32)
    inv = fwd * np.where(k == 0, 1.0, 2.0).astype(np.float32)[None, :, None]
    order = lambda t: t.reshape(2, 32, 4, LAT).transpose(2, 0, 1, 3).reshape(256, LAT).astype(ml_dtypes.bfloat16)
    m = np.arange(KH) - KH // 2
    u = (np.mod(m[:, None] * n[None, :], LAT)).astype(np.float32) * np.float32(2.0 * math.pi / LAT)
    cos, sin = np.cos(u.astype(np.float64)), np.sin(u.astype(np.float64))
    rot = np.concatenate([np.stack([cos, sin], -1), np.stack([-sin, cos], -1)], 0)
    rot = rot.astype(np.float32).reshape(2 * KH, 2 * LAT).astype(ml_dtypes.bfloat16)
    wf, wi = order(fwd), order(inv)
    place = np.zeros((16, 48, 144), np.float32)
    for y in range(4):
        for x in range(4):
            for part in range(3):
                for tap in range(9):
                    place[4 * y + x, 16 * part + tap, 48 * part + 8 * (y + tap // 3) + x + tap % 3] = 1.0
                place[4 * y + x, 16 * part + 9, 48 * part + 6] = 1.0
    return wf, wi, np.ascontiguousarray(wf.T), np.ascontiguousarray(wi.T), rot, np.ascontiguousarray(rot.T), place.astype(ml_dtypes.bfloat16)


def dot(a, b, precision=None):
    return jnp.dot(a, b, preferred_element_type=F32, precision=precision)


def dot_t(a, b, dims, precision=None):
    return lax.dot_general(a, b, (dims, ((), ())), preferred_element_type=F32, precision=precision)


def gelu_pair(v):
    squared = v * v
    t = jnp.tanh(ROOT * (v + CUBE * (squared * v)))
    half = 0.5 * (1.0 + t)
    slope = half + 0.5 * v * (1.0 - t * t) * (ROOT * (1.0 + (3.0 * CUBE) * squared))
    return v * half, slope


def kernel(
    frames_h, taps_h, bias_h, proj_h, w_in_h, b_in_h, gain_h, lbias_h, w1_h, b1_h, w2_h, b2_h, cot_h,
    wf_h, wi_h, wft_h, wit_h, rot_h, rott_h, place_h,
    den_hbm, agw_out, agf_out,
    frames, taps, bias, proj, w_in, b_in, gain, lbias, w1, b1, w2, b2, cot, wf, wi, wft, wit, rot, rott, place,
    ft, fsend, htop, hbot, frecv, rtop, rbot, est, wbig, projt, tp, lat, emb, nrm, istd, den,
    stage, snd, rcv, wc1, wc2, bc, wsend, wrecv, agw, fsnd, fpair, fsum, frcv, agf,
    isem, lsem, fss, frs, hss, hrs, ass, ars, als, wss, wrs, gss, grs, rss, rrs, qss, qrs, pss, prs,
):
    r = lax.axis_index("rows")
    c = lax.axis_index("cols")
    me = r * NC + c
    kg = me // 4
    cg = lax.rem(me, 4)
    core = lax.rem(c, 2)
    chip = me // 2
    partner = me + 1 - 2 * core

    barrier = pltpu.get_barrier_semaphore()

    @pl.loop(1, NR)
    def _(a):
        row = lax.rem(r + a, NR) * NC
        for k in range(NC):
            pl.semaphore_signal(barrier, inc=1, device_id=row + k, device_id_type=pl.DeviceIdType.LOGICAL)

    for k in range(1, NC):
        pl.semaphore_signal(
            barrier, inc=1, device_id=r * NC + lax.rem(c + k, NC), device_id_type=pl.DeviceIdType.LOGICAL)

    inputs = {}
    for i, (src, dst) in enumerate((
            (frames_h, frames), (cot_h, cot), (wi_h, wi), (taps_h, taps), (bias_h, bias), (place_h, place), (proj_h, proj),
            (w1_h, w1), (w2_h, w2), (b1_h, b1), (b2_h, b2), (w_in_h, w_in), (b_in_h, b_in), (gain_h, gain),
            (lbias_h, lbias), (wf_h, wf), (rot_h, rot), (rott_h, rott), (wit_h, wit), (wft_h, wft))):
        inputs[i] = pltpu.make_async_copy(src, dst, isem.at[i])
        inputs[i].start()

    def arrive(*which):
        for i in which:
            inputs[i].wait()

    at_z = [lax.rem(lax.rem(r, 4) + i, 4) * NC for i in range(4)]
    at_yl = [lax.rem(r // 4 + i, 2) * 4 * NC for i in range(2)]
    at_yh = [lax.rem(c // 8 + i, 2) * 8 for i in range(2)]
    at_x = [lax.rem(lax.rem(c // 2, 4) + i, 4) * 2 for i in range(4)]
    at_core = [core, 1 - core]
    at_row = {(z, yl): at_z[z] + at_yl[yl] for z in range(4) for yl in range(2)}
    at_col = {(yh, x, k): at_yh[yh] + at_x[x] + at_core[k] for yh in range(2) for x in range(4) for k in range(2)}

    def every_peer(act, part=slice(None)):
        for z, yl, yh, x, k in PEERS[part]:
            act(at_row[z, yl] + at_col[yh, x, k])

    def every_chip(act):
        for z, yl, yh, x, k in PEERS:
            if k == 0:
                act(at_row[z, yl] + at_col[yh, x, k])

    def remote(src, dst, ss, rs, d):
        return pltpu.make_async_remote_copy(src, dst, ss, rs, device_id=d, device_id_type=pl.DeviceIdType.LOGICAL)

    def batch(ref, ss, rs):
        return remote(ref, ref, ss, rs, partner)

    zero8 = jnp.zeros((8, 128), F32)
    arrive(0)
    for f in range(FRAMES):
        ft[f, 0:8, :] = zero8
        ft[f, 264:272, :] = zero8
        ft[f, 8:264, :] = frames[f].astype(F32)
    for f in range(FRAMES):
        for j in range(NC):
            fsend[j, f] = ft[f, 16 * j + 7 : 16 * j + 31, :].reshape(3, 8, 128).astype(BF16)
        htop[f] = ft[f, 263:271, :].astype(BF16)
        hbot[f] = ft[f, 7:15, :].astype(BF16)

    def put_rows(h, value):
        for k4 in range(4):
            for p in range(2):
                rows = value[k4 * 64 + p * 32 : k4 * 64 + p * 32 + 32, :]
                for g in range(4):
                    stage[k4, pl.ds(8 * g + 2 * h + p, 32, stride=32), :] = rows[:, 128 * g : 128 * g + 128]

    def pack(e):
        for k4 in range(4):
            snd[e, :, :, 128 * k4 : 128 * k4 + 128] = stage[k4].reshape(ND, 8, 128).astype(BF16)

    def send_own(e):
        pltpu.make_async_copy(snd.at[e, me], rcv.at[e, me], als.at[e]).start()

    def send_all(e, part=slice(None)):
        every_peer(lambda d: remote(snd.at[e, d], rcv.at[e, me], ass.at[e], ars.at[e], d).start(), part)

    def recv_all(e):
        pltpu.make_async_copy(snd.at[e, me], rcv.at[e, me], als.at[e]).wait()
        batch(rcv.at[e, pl.ds(0, ND - 1)], ass.at[e], ars.at[e]).wait_recv()

    arrive(1, 2)
    for h in range(ROWS):
        put_rows(h, dot(wi[...], cot[h]) * FACTOR)
    pack(0)

    arrive(3, 4, 5, 6, 7, 8, 9, 10)
    tp[...] = jnp.zeros(tp.shape, F32)
    tp[0:9, :] = taps[...]
    tp[9:10, :] = bias[...]
    whole = tp[...]
    high = whole.astype(BF16)
    rest = whole - high.astype(F32)
    mid = rest.astype(BF16)
    low = (rest - mid.astype(F32)).astype(BF16)
    parts = jnp.concatenate([high, mid, low], axis=0)
    for yx in range(16):
        wbig[32 * yx : 32 * yx + 32, :] = dot_t(parts, place[yx], ((0,), (0,))).astype(BF16)
    row = lax.broadcasted_iota(jnp.int32, (512, 512), 0)
    col = lax.broadcasted_iota(jnp.int32, (512, 512), 1)
    to_yxc = (row == (col & 31) * 16 + (col >> 5)).astype(F32).astype(BF16)
    projt[...] = dot(proj[...], to_yxc).astype(BF16)
    to_phase = (row == (col & 127) * 4 + (col >> 7)).astype(F32).astype(BF16)
    for wc, w in ((wc1, w1), (wc2, w2)):
        wc[...] = jnp.zeros(wc.shape, F32)
        for b in range(2):
            real = w[0, 2 * cg + b]
            imag = w[1, 2 * cg + b]
            lo, hi = 64 * b, 64 * b + 64
            wc[lo:hi, lo:hi] = real
            wc[128 + lo : 128 + hi, 128 + lo : 128 + hi] = real
            wc[lo:hi, 128 + lo : 128 + hi] = imag
            wc[128 + lo : 128 + hi, lo:hi] = -imag
    lanes = pl.ds(pl.multiple_of(cg * 128, 128), 128)
    bias1 = jnp.concatenate([b1[0:1, lanes], b1[1:2, lanes]], axis=1)
    bias2 = jnp.concatenate([b2[0:1, lanes], b2[1:2, lanes]], axis=1)
    for f in range(FRAMES):
        for t in range(4):
            est[f, t, pl.ds(6, 24, stride=8), :] = jnp.ones((24, 128), F32)
            est[f, t, pl.ds(7, 24, stride=8), :] = jnp.zeros((24, 128), F32)

    pl.semaphore_wait(barrier, ND - 1)

    @pl.loop(1, NC)
    def _(i):
        j = lax.rem(c + i, NC)
        remote(fsend.at[j], frecv.at[c], fss, frs, r * NC + j).start()

    own_frames = pltpu.make_async_copy(fsend.at[c], frecv.at[c], lsem.at[1])
    own_frames.start()

    @pl.when(r < NR - 1)
    def _():
        remote(htop, rtop.at[c], hss.at[0], hrs.at[0], (r + 1) * NC).start()

    @pl.when(r > 0)
    def _():
        remote(hbot, rbot.at[c], hss.at[1], hrs.at[1], r * NC - 1).start()

    has_top = jnp.logical_and(c == 0, r > 0)
    has_bot = jnp.logical_and(c == NC - 1, r < NR - 1)

    @pl.when(jnp.logical_not(has_top))
    def _():
        rtop[...] = jnp.zeros(rtop.shape, BF16)

    @pl.when(jnp.logical_not(has_bot))
    def _():
        rbot[...] = jnp.zeros(rbot.shape, BF16)

    send_own(0)
    send_all(0, slice(0, COT_FIRST))

    own_frames.wait()
    batch(frecv.at[pl.ds(0, NC - 1)], fss, frs).wait_recv()

    @pl.when(has_top)
    def _():
        batch(rtop, hss.at[0], hrs.at[0]).wait_recv()

    @pl.when(has_bot)
    def _():
        batch(rbot, hss.at[1], hrs.at[1]).wait_recv()

    send_all(0, slice(COT_FIRST, None))
    split = []
    for g in range(4):
        pieces = []
        for j in range(4):
            v = frecv[4 * g + j].astype(F32)
            up = v[:, 0] + rtop[4 * g + j].astype(F32)
            down = v[:, 2] + rbot[4 * g + j].astype(F32)
            pieces.append(jnp.stack([up, v[:, 1], down], axis=1).reshape(96, 128).astype(BF16))
        split.append(dot(jnp.concatenate(pieces, axis=1), to_phase))
    lane = lax.broadcasted_iota(jnp.int32, (96, 512), 1)
    first = jnp.concatenate([s[:, 0:128] for s in split], axis=1)
    last = jnp.concatenate([s[:, 384:512] for s in split], axis=1)
    before = jnp.where(lane == 0, 0.0, pltpu.roll(last, 1, axis=1))
    after = jnp.where(lane == LAT - 1, 0.0, pltpu.roll(first, LAT - 1, axis=1))
    for t in range(4):
        own = slice(128 * t, 128 * t + 128)
        planes = [before[:, own]] + [split[t][:, 128 * q : 128 * q + 128] for q in range(4)] + [after[:, own]]
        for x, plane in enumerate(planes):
            for f in range(FRAMES):
                est[f, t, pl.ds(x, 24, stride=8), :] = plane[24 * f : 24 * f + 24, :]

    @pl.loop(0, ROWS)
    def _(h):
        for f in range(FRAMES):
            top = pl.multiple_of(32 * h, 32)
            patch = jnp.concatenate([est[f, t, pl.ds(top, 48), :] for t in range(4)], axis=1).astype(BF16)
            hidden = dot(wbig[...], jnp.concatenate([patch, patch, patch], axis=0))
            hidden = jnp.maximum(hidden, 0.0).astype(BF16)
            lat[h, 32 * f : 32 * f + 32, :] = dot(projt[...], hidden).astype(BF16)

    arrive(11, 12, 13, 14, 15)
    for h in range(ROWS):
        embedded = dot_t(lat[h], w_in[...], ((0,), (0,))) + b_in[...]
        emb[h] = embedded
        centered = embedded - jnp.mean(embedded, axis=1, keepdims=True)
        inverse = lax.rsqrt(jnp.mean(centered * centered, axis=1, keepdims=True) + EPS)
        normalized = centered * inverse
        istd[h] = inverse
        nrm[h] = normalized
        normed = (normalized * gain[...] + lbias[...]).astype(BF16)
        put_rows(h, dot(wf[...], normed) * FACTOR)
    pack(1)
    send_own(1)
    send_all(1)

    def to_modes(e):
        x = rcv[e].astype(F32).reshape(2 * LAT, 512).astype(BF16)
        return stacked(dot(rot[...], x) * FACTOR)

    def stacked(v):
        return jnp.concatenate(
            [jnp.concatenate([v[0:KH, 128 * q : 128 * q + 128], v[KH:, 128 * q : 128 * q + 128]], axis=1) for q in range(4)], axis=0)

    def unstacked(v):
        return jnp.concatenate(
            [jnp.concatenate([v[KH * q : KH * q + KH, 128 * p : 128 * p + 128] for q in range(4)], axis=1) for p in range(2)], axis=0)

    def from_modes(e, v, part=slice(None)):
        back = dot(rott[...], unstacked(v).astype(BF16)) * FACTOR
        snd[e] = back.reshape(ND, 8, 512).astype(BF16)
        send_own(e)
        send_all(e, part)

    arrive(16, 17, 18, 19)
    recv_all(0)
    grad = to_modes(0)
    grad_act = dot_t(grad, wc2[...], ((1,), (1,)), HIGHEST)
    recv_all(1)
    coeffs = to_modes(1)
    pre = dot(coeffs, wc1[...], HIGHEST) + bias1
    act, slope = gelu_pair(pre)
    back = grad_act * slope
    from_modes(3, dot_t(back, wc1[...], ((1,), (1,)), HIGHEST))

    half = lax.broadcasted_iota(jnp.int32, (64, 128), 1) < 64

    def weight_grad(left, right):
        g = dot_t(left, right, ((0,), (0,)), HIGHEST)
        real = g[0:128, 0:128] + g[128:256, 128:256]
        imag = g[0:128, 128:256] - g[128:256, 0:128]
        return [jnp.where(half, v[0:64, :], v[64:128, :]) for v in (real, imag)]

    tiles = weight_grad(coeffs, back) + weight_grad(act, grad)
    wsend[...] = jnp.concatenate(tiles, axis=0).reshape(32, 8, 128)
    wrecv[kg] = wsend[kg]

    @pl.loop(1, 32)
    def _(i):
        j = lax.rem(kg + i, 32)
        remote(wsend.at[j], wrecv.at[kg], wss, wrs, 4 * j + cg).start()

    from_modes(2, dot(act, wc2[...], HIGHEST) + bias2, slice(0, OUT_FIRST))

    sum1 = jnp.sum(back, axis=0, keepdims=True)
    sum2 = jnp.sum(grad, axis=0, keepdims=True)
    bc[...] = jnp.zeros(bc.shape, F32)
    for p in range(2):
        bc[p : p + 1, lanes] = sum1[:, 128 * p : 128 * p + 128]
        bc[2 + p : 3 + p, lanes] = sum2[:, 128 * p : 128 * p + 128]

    def get_rows(e, h):
        blocks = []
        for k4 in range(4):
            for q in range(2):
                blocks.append(jnp.concatenate(
                    [stage[k4, pl.ds(8 * g + 2 * h + q, 32, stride=32), :] for g in range(4)], axis=1))
        return jnp.concatenate(blocks, axis=0).astype(BF16)

    def unpack(e):
        for k4 in range(4):
            stage[k4] = rcv[e, :, :, 128 * k4 : 128 * k4 + 128].astype(F32).reshape(8 * ND, 128)

    recv_all(3)
    batch(wrecv.at[pl.ds(0, 31)], wss, wrs).wait_recv()
    agw[core, kg, lax.rem(chip, 2)] = jnp.sum(wrecv[...], axis=0)
    mine = agw.at[core, kg, lax.rem(chip, 2)]
    every_chip(lambda d: remote(mine, mine, gss, grs, d).start())

    unpack(3)
    sums = [jnp.zeros((1, WIDTH), F32) for _ in range(3)]
    weight = jnp.zeros((128, WIDTH), F32)
    for h in range(ROWS):
        gn = dot(wft[...], get_rows(3, h)) * FACTOR
        normalized = nrm[h]
        sums[1] = sums[1] + jnp.sum(gn * normalized, axis=0, keepdims=True)
        sums[2] = sums[2] + jnp.sum(gn, axis=0, keepdims=True)
        scaled = gn * gain[...]
        ge = cot[h].astype(F32) + istd[h] * (
            scaled
            - jnp.mean(scaled, axis=1, keepdims=True)
            - normalized * jnp.mean(scaled * normalized, axis=1, keepdims=True))
        sums[0] = sums[0] + jnp.sum(ge, axis=0, keepdims=True)
        weight = weight + dot(lat[h], ge.astype(BF16))

    for a in range(32):
        for b in range(4):
            own = slice(128 * b, 128 * b + 128)
            at = (b % 2, 2 * a + b // 2)
            fsnd[at[0], at[1], 0:4, :] = weight[4 * a : 4 * a + 4, own]
            if a < 3:
                fsnd[at[0], at[1], 4:5, :] = sums[a][:, own]
            elif a < 7:
                fsnd[at[0], at[1], 4:5, :] = bc[a - 3 : a - 2, own]
            else:
                fsnd[at[0], at[1], 4:5, :] = jnp.zeros((1, 128), F32)
            fsnd[at[0], at[1], 5:8, :] = jnp.zeros((3, 128), F32)
    remote(fsnd.at[1 - core], fpair, pss.at[0], prs.at[0], partner).start()
    batch(fpair, pss.at[0], prs.at[0]).wait_recv()
    fsum[...] = fsnd[core] + fpair[...]
    frcv[chip] = fsum[chip]
    every_chip(lambda d: remote(fsum.at[d // 2], frcv.at[chip], rss, rrs, d).start())

    send_all(2, slice(OUT_FIRST, None))

    batch(frcv.at[pl.ds(0, 63)], rss, rrs).wait_recv()
    agf[core, chip] = jnp.sum(frcv[...], axis=0)
    every_chip(lambda d: remote(agf.at[core, chip], agf.at[core, chip], qss, qrs, d).start())

    recv_all(2)
    unpack(2)
    for h in range(ROWS):
        den[h] = (emb[h] + dot(wit[...], get_rows(2, h)) * FACTOR).astype(BF16)
        pltpu.make_async_copy(den.at[h], den_hbm.at[h], lsem.at[2 + h]).start()

    batch(frcv.at[pl.ds(0, 63)], gss, grs).wait_recv()
    remote(agw.at[core], agw.at[core], pss.at[1], prs.at[1], partner).start()
    batch(frcv.at[pl.ds(0, 63)], qss, qrs).wait_recv()
    remote(agf.at[core], agf.at[core], pss.at[2], prs.at[2], partner).start()
    batch(agw.at[0], pss.at[1], prs.at[1]).wait_recv()
    agw_copy = pltpu.make_async_copy(agw, agw_out, lsem.at[6])
    agw_copy.start()
    batch(agf.at[0], pss.at[2], prs.at[2]).wait_recv()
    agf_copy = pltpu.make_async_copy(agf, agf_out, lsem.at[7])
    agf_copy.start()

    agw_copy.wait()
    agf_copy.wait()
    for h in range(ROWS):
        pltpu.make_async_copy(den.at[h], den_hbm.at[h], lsem.at[2 + h]).wait()
    batch(frecv.at[pl.ds(0, NC - 1)], fss, frs).wait_send()

    @pl.when(r < NR - 1)
    def _():
        batch(htop, hss.at[0], hrs.at[0]).wait_send()

    @pl.when(r > 0)
    def _():
        batch(hbot, hss.at[1], hrs.at[1]).wait_send()

    for e in range(4):
        batch(rcv.at[e, pl.ds(0, ND - 1)], ass.at[e], ars.at[e]).wait_send()
    batch(wrecv.at[pl.ds(0, 31)], wss, wrs).wait_send()
    batch(fpair, pss.at[0], prs.at[0]).wait_send()
    batch(agw.at[0], pss.at[1], prs.at[1]).wait_send()
    batch(agf.at[0], pss.at[2], prs.at[2]).wait_send()
    for ss, rs in ((gss, grs), (rss, rrs), (qss, qrs)):
        batch(frcv.at[pl.ds(0, 63)], ss, rs).wait_send()


def finish(den_in, agw, agf, den_out, gwin, gbin, ggain, gbias, gw1, gb1, gw2, gb2, sem):
    outs = [pltpu.make_async_copy(den_in.at[h], den_out.at[h], sem.at[h]) for h in range(ROWS)]
    for copy in outs:
        copy.start()
    for w, gw in enumerate((gw1, gw2)):
        for p in range(2):
            for g in range(4):
                v = agw[g % 2, 16 * w + 8 * p : 16 * w + 8 * p + 8, g // 2].reshape(64, 128)
                gw[p, 2 * g] = v[:, 0:64]
                gw[p, 2 * g + 1] = v[:, 64:128]
    small = (gbin, ggain, gbias)
    for b in range(4):
        own = slice(128 * b, 128 * b + 128)
        for a in range(32):
            gwin[4 * a : 4 * a + 4, own] = agf[b % 2, 2 * a + b // 2, 0:4, :]
        for a in range(3):
            small[a][:, own] = agf[b % 2, 2 * a + b // 2, 4:5, :]
        for a in range(2):
            gb1[a : a + 1, own] = agf[b % 2, 2 * (a + 3) + b // 2, 4:5, :]
            gb2[a : a + 1, own] = agf[b % 2, 2 * (a + 5) + b // 2, 4:5, :]
    for copy in outs:
        copy.wait()


def body(frames, enc_taps, enc_bias, enc_proj, w_in, b_in, ln_gain, ln_bias, spec_w1, spec_b1, spec_w2, spec_b2, cotangent):
    vmem = pl.BlockSpec(memory_space=pltpu.VMEM)
    hbm = pl.BlockSpec(memory_space=pltpu.HBM)
    anywhere = pl.BlockSpec(memory_space=pl.ANY)
    shape = jax.ShapeDtypeStruct
    dma = pltpu.SemaphoreType.DMA
    operands = (
        frames, enc_taps, enc_bias.reshape(1, -1), enc_proj.T, w_in, b_in.reshape(1, -1), ln_gain.reshape(1, -1),
        ln_bias.reshape(1, -1), spec_w1, spec_b1, spec_w2, spec_b2, cotangent) + tuple(jnp.asarray(t) for t in tables())
    den, agw, agf = pl.pallas_call(
        kernel,
        out_shape=(shape((ROWS, LAT, WIDTH), BF16), shape((2, 32, 2, 8, 128), F32), shape((2, 64, 8, 128), F32)),
        in_specs=[hbm] * 20,
        out_specs=(anywhere, anywhere, anywhere),
        scratch_shapes=[pltpu.VMEM(x.shape, x.dtype) for x in operands] + [
            pltpu.VMEM((FRAMES, 272, 128), F32),
            pltpu.VMEM((NC, FRAMES, 3, 8, 128), BF16),
            pltpu.VMEM((FRAMES, 8, 128), BF16),
            pltpu.VMEM((FRAMES, 8, 128), BF16),
            pltpu.VMEM((NC, FRAMES, 3, 8, 128), BF16),
            pltpu.VMEM((NC, FRAMES, 8, 128), BF16),
            pltpu.VMEM((NC, FRAMES, 8, 128), BF16),
            pltpu.VMEM((FRAMES, 4, 192, 128), F32),
            pltpu.VMEM((512, 144), BF16),
            pltpu.VMEM((32, 512), BF16),
            pltpu.VMEM((16, 32), F32),
            pltpu.VMEM((ROWS, 128, LAT), BF16),
            pltpu.VMEM((ROWS, LAT, WIDTH), F32),
            pltpu.VMEM((ROWS, LAT, WIDTH), F32),
            pltpu.VMEM((ROWS, LAT, 1), F32),
            pltpu.VMEM((ROWS, LAT, WIDTH), BF16),
            pltpu.VMEM((4, 8 * ND, 128), F32),
            pltpu.VMEM((4, ND, 8, 512), BF16),
            pltpu.VMEM((4, ND, 8, 512), BF16),
            pltpu.VMEM((256, 256), F32),
            pltpu.VMEM((256, 256), F32),
            pltpu.VMEM((8, WIDTH), F32),
            pltpu.VMEM((32, 8, 128), F32),
            pltpu.VMEM((32, 8, 128), F32),
            pltpu.VMEM((2, 32, 2, 8, 128), F32),
            pltpu.VMEM((2, 64, 8, 128), F32),
            pltpu.VMEM((64, 8, 128), F32),
            pltpu.VMEM((64, 8, 128), F32),
            pltpu.VMEM((64, 8, 128), F32),
            pltpu.VMEM((2, 64, 8, 128), F32),
            dma((20,)), dma((8,)), dma(()), dma(()), dma((2,)), dma((2,)), dma((4,)), dma((4,)), dma((4,)),
            dma(()), dma(()), dma(()), dma(()), dma(()), dma(()), dma(()), dma(()), dma((3,)), dma((3,)),
        ],
        compiler_params=pltpu.CompilerParams(
            collective_id=0, has_side_effects=True, vmem_limit_bytes=VMEM_LIMIT),
        name="step",
    )(*(pltpu.with_memory_space_constraint(x, pltpu.HBM) for x in operands))
    den, gwin, gbin, ggain, gbias, gw1, gb1, gw2, gb2 = pl.pallas_call(
        finish,
        out_shape=(
            shape((ROWS, LAT, WIDTH), BF16), shape((128, WIDTH), F32), shape((1, WIDTH), F32), shape((1, WIDTH), F32),
            shape((1, WIDTH), F32), shape((2, 8, 64, 64), F32), shape((2, WIDTH), F32), shape((2, 8, 64, 64), F32),
            shape((2, WIDTH), F32)),
        in_specs=[vmem] * 3,
        out_specs=(hbm,) + (vmem,) * 8,
        scratch_shapes=[dma((ROWS,))],
        compiler_params=pltpu.CompilerParams(vmem_limit_bytes=16 * 1024 * 1024),
        name="finish",
    )(den, agw, agf)
    return (den, gwin, gbin.reshape(-1), ggain.reshape(-1), gbias.reshape(-1), gw1, gb1, gw2, gb2)


def solution(mesh):
    return jax.shard_map(
        body,
        mesh=mesh,
        in_specs=(P(None, "rows", "cols"),) + (P(),) * 11 + (P(("rows", "cols"), None, None),),
        out_specs=(P(("rows", "cols"), None, None),) + (P(),) * 8,
        check_vma=False,
    )
```

```python
import itertools
import math
import random

import jax
import jax.numpy as jnp
import ml_dtypes
import numpy as np
from jax import lax
from jax.experimental import pallas as pl
from jax.experimental.pallas import tpu as pltpu
from jax.sharding import PartitionSpec as P

F32 = jnp.float32
BF16 = jnp.bfloat16
HIGHEST = lax.Precision.HIGHEST

NR, NC = 8, 16
ND = NR * NC
LAT = 512
WIDTH = 512
KH = 128
ROWS = 4
FRAMES = 4


def far_first():
    offsets = [o for o in itertools.product(range(4), range(2), range(2), range(4), range(2)) if any(o)]
    random.Random(1).shuffle(offsets)
    y_hops = {(0, 0): 0, (1, 0): 1, (0, 1): 2, (1, 1): 1}
    return sorted(offsets, key=lambda o: -(min(o[0], 4 - o[0]) + min(o[3], 4 - o[3]) + y_hops[o[1], o[2]]))


PEERS = far_first()
OUT_FIRST = 24
OUT_SECOND = 24
SUMS_AT = 4
VMEM_LIMIT = 44 * 1024 * 1024
EPS = 1e-05
FACTOR = LAT ** (-0.5)
CUBE = 0.044715
ROOT = math.sqrt(2.0 / math.pi)


def tables():
    n = np.arange(LAT)
    k = np.arange(ND)
    angle = ((k[:, None] * n[None, :]) % LAT).astype(np.float32) * np.float32(2.0 * math.pi / LAT)
    fwd = np.stack([np.cos(angle.astype(np.float64)), -np.sin(angle.astype(np.float64))]).astype(np.float32)
    inv = fwd * np.where(k == 0, 1.0, 2.0).astype(np.float32)[None, :, None]
    order = lambda t: t.reshape(2, 32, 4, LAT).transpose(2, 0, 1, 3).reshape(256, LAT).astype(ml_dtypes.bfloat16)
    m = np.arange(KH) - KH // 2
    u = (np.mod(m[:, None] * n[None, :], LAT)).astype(np.float32) * np.float32(2.0 * math.pi / LAT)
    cos, sin = np.cos(u.astype(np.float64)), np.sin(u.astype(np.float64))
    rot = np.concatenate([np.stack([cos, sin], -1), np.stack([-sin, cos], -1)], 0)
    rot = rot.astype(np.float32).reshape(2 * KH, 2 * LAT).astype(ml_dtypes.bfloat16)
    wf, wi = order(fwd), order(inv)
    place = np.zeros((16, 48, 144), np.float32)
    for y in range(4):
        for x in range(4):
            for part in range(3):
                for tap in range(9):
                    place[4 * y + x, 16 * part + tap, 48 * part + 8 * (y + tap // 3) + x + tap % 3] = 1.0
                place[4 * y + x, 16 * part + 9, 48 * part + 6] = 1.0
    return wf, wi, np.ascontiguousarray(wf.T), np.ascontiguousarray(wi.T), rot, np.ascontiguousarray(rot.T), place.astype(ml_dtypes.bfloat16)


def dot(a, b, precision=None):
    return jnp.dot(a, b, preferred_element_type=F32, precision=precision)


def dot_t(a, b, dims, precision=None):
    return lax.dot_general(a, b, (dims, ((), ())), preferred_element_type=F32, precision=precision)


def gelu_pair(v):
    squared = v * v
    t = jnp.tanh(ROOT * (v + CUBE * (squared * v)))
    half = 0.5 * (1.0 + t)
    slope = half + 0.5 * v * (1.0 - t * t) * (ROOT * (1.0 + (3.0 * CUBE) * squared))
    return v * half, slope


def kernel(
    frames_h, taps_h, bias_h, proj_h, w_in_h, b_in_h, gain_h, lbias_h, w1_h, b1_h, w2_h, b2_h, cot_h,
    wf_h, wi_h, wft_h, wit_h, rot_h, rott_h, place_h,
    den_hbm, agw_out, agf_out, agt_out,
    frames, taps, bias, proj, w_in, b_in, gain, lbias, w1, b1, w2, b2, cot, wf, wi, wft, wit, rot, rott, place,
    ft, fsend, htop, hbot, frecv, rtop, rbot, est, wbig, projt, tp, lat, emb, nrm, istd, den,
    stage, snd, rcv, wc1, wc2, bc, wsend, wrecv, agw, fsnd, fpair, fsum, frcv, agf, tiny, tpair, tsum, trcv, agt,
    isem, lsem, fss, frs, hss, hrs, ass, ars, als, wss, wrs, gss, grs, rss, rrs, qss, qrs, pss, prs, tss, trs, uss, urs,
):
    r = lax.axis_index("rows")
    c = lax.axis_index("cols")
    me = r * NC + c
    kg = me // 4
    cg = lax.rem(me, 4)
    core = lax.rem(c, 2)
    chip = me // 2
    partner = me + 1 - 2 * core
    owner = (13 + 24 * core, 50 - 24 * core)

    barrier = pltpu.get_barrier_semaphore()

    @pl.loop(1, NR)
    def _(a):
        row = lax.rem(r + a, NR) * NC
        for k in range(NC):
            pl.semaphore_signal(barrier, inc=1, device_id=row + k, device_id_type=pl.DeviceIdType.LOGICAL)

    for k in range(1, NC):
        pl.semaphore_signal(
            barrier, inc=1, device_id=r * NC + lax.rem(c + k, NC), device_id_type=pl.DeviceIdType.LOGICAL)

    inputs = {}
    for i, (src, dst) in enumerate((
            (frames_h, frames), (cot_h, cot), (wi_h, wi), (taps_h, taps), (bias_h, bias), (place_h, place), (proj_h, proj),
            (w1_h, w1), (w2_h, w2), (b1_h, b1), (b2_h, b2), (w_in_h, w_in), (b_in_h, b_in), (gain_h, gain),
            (lbias_h, lbias), (wf_h, wf), (rot_h, rot), (rott_h, rott), (wit_h, wit), (wft_h, wft))):
        inputs[i] = pltpu.make_async_copy(src, dst, isem.at[i])
        inputs[i].start()

    def arrive(*which):
        for i in which:
            inputs[i].wait()

    at_z = [lax.rem(lax.rem(r, 4) + i, 4) * NC for i in range(4)]
    at_yl = [lax.rem(r // 4 + i, 2) * 4 * NC for i in range(2)]
    at_yh = [lax.rem(c // 8 + i, 2) * 8 for i in range(2)]
    at_x = [lax.rem(lax.rem(c // 2, 4) + i, 4) * 2 for i in range(4)]
    at_core = [core, 1 - core]
    at_row = {(z, yl): at_z[z] + at_yl[yl] for z in range(4) for yl in range(2)}
    at_col = {(yh, x, k): at_yh[yh] + at_x[x] + at_core[k] for yh in range(2) for x in range(4) for k in range(2)}

    def every_peer(act, part=slice(None)):
        for z, yl, yh, x, k in PEERS[part]:
            act(at_row[z, yl] + at_col[yh, x, k])

    def every_chip(act):
        for z, yl, yh, x, k in PEERS:
            if k == 0:
                act(at_row[z, yl] + at_col[yh, x, k])

    def remote(src, dst, ss, rs, d):
        return pltpu.make_async_remote_copy(src, dst, ss, rs, device_id=d, device_id_type=pl.DeviceIdType.LOGICAL)

    def batch(ref, ss, rs):
        return remote(ref, ref, ss, rs, partner)

    zero8 = jnp.zeros((8, 128), F32)
    arrive(0)
    for f in range(FRAMES):
        ft[f, 0:8, :] = zero8
        ft[f, 264:272, :] = zero8
        ft[f, 8:264, :] = frames[f].astype(F32)
    for f in range(FRAMES):
        for j in range(NC):
            fsend[j, f] = ft[f, 16 * j + 7 : 16 * j + 31, :].reshape(3, 8, 128).astype(BF16)
        htop[f] = ft[f, 263:271, :].astype(BF16)
        hbot[f] = ft[f, 7:15, :].astype(BF16)

    def put_rows(h, value):
        for k4 in range(4):
            for p in range(2):
                rows = value[k4 * 64 + p * 32 : k4 * 64 + p * 32 + 32, :]
                for g in range(4):
                    stage[k4, pl.ds(8 * g + 2 * h + p, 32, stride=32), :] = rows[:, 128 * g : 128 * g + 128]

    def pack(e):
        for k4 in range(4):
            snd[e, :, :, 128 * k4 : 128 * k4 + 128] = stage[k4].reshape(ND, 8, 128).astype(BF16)

    def send_own(e):
        pltpu.make_async_copy(snd.at[e, me], rcv.at[e, me], als.at[e]).start()

    def send_all(e, part=slice(None)):
        every_peer(lambda d: remote(snd.at[e, d], rcv.at[e, me], ass.at[e], ars.at[e], d).start(), part)

    def recv_all(e):
        pltpu.make_async_copy(snd.at[e, me], rcv.at[e, me], als.at[e]).wait()
        batch(rcv.at[e, pl.ds(0, ND - 1)], ass.at[e], ars.at[e]).wait_recv()

    arrive(1, 2)
    for h in range(ROWS):
        put_rows(h, dot(wi[...], cot[h]) * FACTOR)
    pack(0)

    arrive(3, 4, 5, 6, 7, 8, 9, 10)
    tp[...] = jnp.zeros(tp.shape, F32)
    tp[0:9, :] = taps[...]
    tp[9:10, :] = bias[...]
    whole = tp[...]
    high = whole.astype(BF16)
    rest = whole - high.astype(F32)
    mid = rest.astype(BF16)
    low = (rest - mid.astype(F32)).astype(BF16)
    parts = jnp.concatenate([high, mid, low], axis=0)
    for yx in range(16):
        wbig[32 * yx : 32 * yx + 32, :] = dot_t(parts, place[yx], ((0,), (0,))).astype(BF16)
    row = lax.broadcasted_iota(jnp.int32, (512, 512), 0)
    col = lax.broadcasted_iota(jnp.int32, (512, 512), 1)
    to_yxc = (row == (col & 31) * 16 + (col >> 5)).astype(F32).astype(BF16)
    projt[...] = dot(proj[...], to_yxc).astype(BF16)
    to_phase = (row == (col & 127) * 4 + (col >> 7)).astype(F32).astype(BF16)
    for wc, w in ((wc1, w1), (wc2, w2)):
        wc[...] = jnp.zeros(wc.shape, BF16)
        for b in range(2):
            lo, hi = 64 * b, 64 * b + 64
            for p in range(2):
                whole = w[p, 2 * cg + b]
                high = whole.astype(BF16)
                for i, v in enumerate((high, (whole - high.astype(F32)).astype(BF16))):
                    if p == 0:
                        wc[i, lo:hi, lo:hi] = v
                        wc[i, 128 + lo : 128 + hi, 128 + lo : 128 + hi] = v
                    else:
                        wc[i, lo:hi, 128 + lo : 128 + hi] = v
                        wc[i, 128 + lo : 128 + hi, lo:hi] = -v
    lanes = pl.ds(pl.multiple_of(cg * 128, 128), 128)
    bias1 = jnp.concatenate([b1[0:1, lanes], b1[1:2, lanes]], axis=1)
    bias2 = jnp.concatenate([b2[0:1, lanes], b2[1:2, lanes]], axis=1)
    for f in range(FRAMES):
        for t in range(4):
            est[f, t, pl.ds(6, 24, stride=8), :] = jnp.ones((24, 128), F32)
            est[f, t, pl.ds(7, 24, stride=8), :] = jnp.zeros((24, 128), F32)

    pl.semaphore_wait(barrier, ND - 1)

    for j in [at_col[yh, x, k] for z, yl, yh, x, k in PEERS if z == yl == 0]:
        remote(fsend.at[j], frecv.at[c], fss, frs, r * NC + j).start()

    own_frames = pltpu.make_async_copy(fsend.at[c], frecv.at[c], lsem.at[1])
    own_frames.start()

    @pl.when(r < NR - 1)
    def _():
        remote(htop, rtop.at[c], hss.at[0], hrs.at[0], (r + 1) * NC).start()

    @pl.when(r > 0)
    def _():
        remote(hbot, rbot.at[c], hss.at[1], hrs.at[1], r * NC - 1).start()

    has_top = jnp.logical_and(c == 0, r > 0)
    has_bot = jnp.logical_and(c == NC - 1, r < NR - 1)

    @pl.when(jnp.logical_not(has_top))
    def _():
        rtop[...] = jnp.zeros(rtop.shape, BF16)

    @pl.when(jnp.logical_not(has_bot))
    def _():
        rbot[...] = jnp.zeros(rbot.shape, BF16)

    send_own(0)

    own_frames.wait()
    batch(frecv.at[pl.ds(0, NC - 1)], fss, frs).wait_recv()

    @pl.when(has_top)
    def _():
        batch(rtop, hss.at[0], hrs.at[0]).wait_recv()

    @pl.when(has_bot)
    def _():
        batch(rbot, hss.at[1], hrs.at[1]).wait_recv()

    send_all(0)
    split = []
    for g in range(4):
        pieces = []
        for j in range(4):
            v = frecv[4 * g + j].astype(F32)
            up = v[:, 0] + rtop[4 * g + j].astype(F32)
            down = v[:, 2] + rbot[4 * g + j].astype(F32)
            pieces.append(jnp.stack([up, v[:, 1], down], axis=1).reshape(96, 128).astype(BF16))
        split.append(dot(jnp.concatenate(pieces, axis=1), to_phase))
    lane = lax.broadcasted_iota(jnp.int32, (96, 512), 1)
    first = jnp.concatenate([s[:, 0:128] for s in split], axis=1)
    last = jnp.concatenate([s[:, 384:512] for s in split], axis=1)
    before = jnp.where(lane == 0, 0.0, pltpu.roll(last, 1, axis=1))
    after = jnp.where(lane == LAT - 1, 0.0, pltpu.roll(first, LAT - 1, axis=1))
    for t in range(4):
        own = slice(128 * t, 128 * t + 128)
        planes = [before[:, own]] + [split[t][:, 128 * q : 128 * q + 128] for q in range(4)] + [after[:, own]]
        for x, plane in enumerate(planes):
            for f in range(FRAMES):
                est[f, t, pl.ds(x, 24, stride=8), :] = plane[24 * f : 24 * f + 24, :]

    @pl.loop(0, ROWS)
    def _(h):
        for f in range(FRAMES):
            top = pl.multiple_of(32 * h, 32)
            patch = jnp.concatenate([est[f, t, pl.ds(top, 48), :] for t in range(4)], axis=1).astype(BF16)
            hidden = dot(wbig[...], jnp.concatenate([patch, patch, patch], axis=0))
            hidden = jnp.maximum(hidden, 0.0).astype(BF16)
            lat[h, 32 * f : 32 * f + 32, :] = dot(projt[...], hidden).astype(BF16)

    arrive(11, 12, 13, 14, 15)
    for h in range(ROWS):
        embedded = dot_t(lat[h], w_in[...], ((0,), (0,))) + b_in[...]
        emb[h] = embedded
        centered = embedded - jnp.mean(embedded, axis=1, keepdims=True)
        inverse = lax.rsqrt(jnp.mean(centered * centered, axis=1, keepdims=True) + EPS)
        normalized = centered * inverse
        istd[h] = inverse
        nrm[h] = normalized
        normed = (normalized * gain[...] + lbias[...]).astype(BF16)
        put_rows(h, dot(wf[...], normed) * FACTOR)
    pack(1)
    send_own(1)
    send_all(1)

    def to_modes(e):
        x = rcv[e].reshape(2 * LAT, 512)
        return stacked(dot(rot[...], x) * FACTOR)

    def stacked(v):
        return jnp.concatenate(
            [jnp.concatenate([v[0:KH, 128 * q : 128 * q + 128], v[KH:, 128 * q : 128 * q + 128]], axis=1) for q in range(4)], axis=0)

    def unstacked(v):
        return jnp.concatenate(
            [jnp.concatenate([v[KH * q : KH * q + KH, 128 * p : 128 * p + 128] for q in range(4)], axis=1) for p in range(2)], axis=0)

    def to_back(e, v):
        back = dot(rott[...], unstacked(v).astype(BF16)) * FACTOR
        snd[e] = back.reshape(ND, 8, 512).astype(BF16)

    def dot3(v, wc, side=0):
        high = v.astype(BF16)
        low = (v - high.astype(F32)).astype(BF16)
        dims = ((1,), (side,))
        return dot_t(high, wc[0], dims) + (dot_t(high, wc[1], dims) + dot_t(low, wc[0], dims))

    arrive(16, 17, 18, 19)
    recv_all(0)
    grad = to_modes(0)
    grad_act = dot3(grad, wc2, 1)
    recv_all(1)
    coeffs = to_modes(1)
    pre = dot3(coeffs, wc1) + bias1
    act, slope = gelu_pair(pre)
    back = grad_act * slope
    to_back(3, dot3(back, wc1, 1))
    send_own(3)
    send_all(3)

    half = lax.broadcasted_iota(jnp.int32, (64, 128), 1) < 64

    def weight_grad(left, right):
        g = dot_t(left, right, ((0,), (0,)), HIGHEST)
        real = g[0:128, 0:128] + g[128:256, 128:256]
        imag = g[0:128, 128:256] - g[128:256, 0:128]
        return [jnp.where(half, v[0:64, :], v[64:128, :]) for v in (real, imag)]

    tiles = weight_grad(coeffs, back) + weight_grad(act, grad)
    wsend[...] = jnp.concatenate(tiles, axis=0).reshape(32, 8, 128)
    wrecv[kg] = wsend[kg]

    @pl.loop(1, 32)
    def _(i):
        j = lax.rem(kg + i, 32)
        remote(wsend.at[j], wrecv.at[kg], wss, wrs, 4 * j + cg).start()

    to_back(2, dot3(act, wc2) + bias2)

    sum1 = jnp.sum(back, axis=0, keepdims=True)
    sum2 = jnp.sum(grad, axis=0, keepdims=True)
    bc[...] = jnp.zeros(bc.shape, F32)
    for p in range(2):
        bc[p : p + 1, lanes] = sum1[:, 128 * p : 128 * p + 128]
        bc[2 + p : 3 + p, lanes] = sum2[:, 128 * p : 128 * p + 128]

    def get_rows(e, h):
        blocks = []
        for k4 in range(4):
            for q in range(2):
                blocks.append(jnp.concatenate(
                    [stage[k4, pl.ds(8 * g + 2 * h + q, 32, stride=32), :] for g in range(4)], axis=1))
        return jnp.concatenate(blocks, axis=0).astype(BF16)

    def unpack(e):
        for k4 in range(4):
            stage[k4] = rcv[e, :, :, 128 * k4 : 128 * k4 + 128].astype(F32).reshape(8 * ND, 128)

    recv_all(3)
    send_own(2)
    send_all(2, slice(0, OUT_FIRST))
    unpack(3)
    mine = agw.at[core, kg, lax.rem(chip, 2)]
    wide = trcv.at[0, pl.ds(0, 63)]

    def send_spectral_sums():
        batch(wrecv.at[pl.ds(0, 31)], wss, wrs).wait_recv()
        agw[core, kg, lax.rem(chip, 2)] = jnp.sum(wrecv[...], axis=0)
        every_chip(lambda d: remote(mine, mine, gss, grs, d).start())

    scaled_gain = gain[...] * FACTOR
    sums = [jnp.zeros((1, WIDTH), F32) for _ in range(3)]
    weight = jnp.zeros((128, WIDTH), F32)
    for h in range(ROWS):
        if SUMS_AT == h:
            send_spectral_sums()
        gn = dot(wft[...], get_rows(3, h))
        normalized = nrm[h]
        sums[1] = sums[1] + jnp.sum(gn * normalized, axis=0, keepdims=True)
        sums[2] = sums[2] + jnp.sum(gn, axis=0, keepdims=True)
        scaled = gn * scaled_gain
        ge = cot[h].astype(F32) + istd[h] * (
            scaled
            - jnp.mean(scaled, axis=1, keepdims=True)
            - normalized * jnp.mean(scaled * normalized, axis=1, keepdims=True))
        sums[0] = sums[0] + jnp.sum(ge, axis=0, keepdims=True)
        weight = weight + dot(lat[h], ge.astype(BF16))
    sums = [sums[0], sums[1] * FACTOR, sums[2] * FACTOR]

    for b in range(4):
        own = slice(128 * b, 128 * b + 128)
        for a in range(32):
            fsnd[b % 2, 2 * a + b // 2] = weight[4 * a : 4 * a + 4, own]
        tiny[b % 2, b // 2] = jnp.concatenate([v[:, own] for v in sums] + [bc[0:4, own], jnp.zeros((1, 128), F32)], axis=0)
    remote(fsnd.at[1 - core], fpair, pss.at[0], prs.at[0], partner).start()
    remote(tiny.at[1 - core], tpair, pss.at[3], prs.at[3], partner).start()
    batch(fpair, pss.at[0], prs.at[0]).wait_recv()
    fsum[...] = fsnd[core] + fpair[...]
    frcv[chip] = fsum[chip]
    every_chip(lambda d: remote(fsum.at[d // 2], frcv.at[chip], rss, rrs, d).start())
    batch(tpair, pss.at[3], prs.at[3]).wait_recv()
    tsum[...] = tiny[core] + tpair[...]
    for t in range(2):
        trcv[t, chip] = tsum[t]

        @pl.when(chip != owner[t])
        def _():
            remote(tsum.at[t], trcv.at[t, chip], tss.at[t], trs.at[t], 2 * owner[t] + core).start()

    send_all(2, slice(OUT_FIRST, OUT_SECOND))
    if SUMS_AT == 4:
        send_spectral_sums()

    batch(frcv.at[pl.ds(0, 63)], rss, rrs).wait_recv()
    agf[core, chip] = jnp.sum(frcv[...], axis=0)
    every_chip(lambda d: remote(agf.at[core, chip], agf.at[core, chip], qss, qrs, d).start())
    for t in range(2):

        @pl.when(chip == owner[t])
        def _():
            batch(trcv.at[t, pl.ds(0, 63)], tss.at[t], trs.at[t]).wait_recv()
            agt[core, t] = jnp.sum(trcv[t], axis=0)
            every_chip(lambda d: remote(agt.at[core, t], agt.at[core, t], uss.at[t], urs.at[t], d).start())

    if SUMS_AT == 5:
        send_spectral_sums()
    send_all(2, slice(OUT_SECOND, None))

    batch(wide, gss, grs).wait_recv()
    remote(agw.at[core], agw.at[core], pss.at[1], prs.at[1], partner).start()
    batch(frcv.at[pl.ds(0, 63)], qss, qrs).wait_recv()
    remote(agf.at[core], agf.at[core], pss.at[2], prs.at[2], partner).start()
    for t in range(2):

        @pl.when(chip != owner[t])
        def _():
            batch(agt.at[core, t], uss.at[t], urs.at[t]).wait_recv()

    remote(agt.at[core], agt.at[core], pss.at[4], prs.at[4], partner).start()
    recv_all(2)
    unpack(2)
    for h in range(ROWS):
        den[h] = (emb[h] + dot(wit[...], get_rows(2, h)) * FACTOR).astype(BF16)
        pltpu.make_async_copy(den.at[h], den_hbm.at[h], lsem.at[2 + h]).start()

    batch(agw.at[0], pss.at[1], prs.at[1]).wait_recv()
    agw_copy = pltpu.make_async_copy(agw, agw_out, lsem.at[6])
    agw_copy.start()
    batch(agf.at[0], pss.at[2], prs.at[2]).wait_recv()
    agf_copy = pltpu.make_async_copy(agf, agf_out, lsem.at[7])
    agf_copy.start()
    batch(agt.at[0], pss.at[4], prs.at[4]).wait_recv()
    agt_copy = pltpu.make_async_copy(agt, agt_out, lsem.at[0])
    agt_copy.start()

    agw_copy.wait()
    agf_copy.wait()
    agt_copy.wait()
    for h in range(ROWS):
        pltpu.make_async_copy(den.at[h], den_hbm.at[h], lsem.at[2 + h]).wait()
    batch(frecv.at[pl.ds(0, NC - 1)], fss, frs).wait_send()

    @pl.when(r < NR - 1)
    def _():
        batch(htop, hss.at[0], hrs.at[0]).wait_send()

    @pl.when(r > 0)
    def _():
        batch(hbot, hss.at[1], hrs.at[1]).wait_send()

    for e in range(4):
        batch(rcv.at[e, pl.ds(0, ND - 1)], ass.at[e], ars.at[e]).wait_send()
    batch(wrecv.at[pl.ds(0, 31)], wss, wrs).wait_send()
    batch(fpair, pss.at[0], prs.at[0]).wait_send()
    batch(agw.at[0], pss.at[1], prs.at[1]).wait_send()
    batch(agf.at[0], pss.at[2], prs.at[2]).wait_send()
    batch(tpair, pss.at[3], prs.at[3]).wait_send()
    batch(agt.at[0], pss.at[4], prs.at[4]).wait_send()
    batch(wide, gss, grs).wait_send()
    batch(frcv.at[pl.ds(0, 63)], rss, rrs).wait_send()
    batch(frcv.at[pl.ds(0, 63)], qss, qrs).wait_send()
    for t in range(2):

        @pl.when(chip != owner[t])
        def _():
            batch(tsum.at[t], tss.at[t], trs.at[t]).wait_send()

        @pl.when(chip == owner[t])
        def _():
            batch(trcv.at[t, pl.ds(0, 63)], uss.at[t], urs.at[t]).wait_send()


def finish(den_in, agw, agf, agt, den_out, gwin, gbin, ggain, gbias, gw1, gb1, gw2, gb2, sem):
    outs = [pltpu.make_async_copy(den_in.at[h], den_out.at[h], sem.at[h]) for h in range(ROWS)]
    for copy in outs:
        copy.start()
    for w, gw in enumerate((gw1, gw2)):
        for p in range(2):
            for g in range(4):
                v = agw[g % 2, 16 * w + 8 * p : 16 * w + 8 * p + 8, g // 2].reshape(64, 128)
                gw[p, 2 * g] = v[:, 0:64]
                gw[p, 2 * g + 1] = v[:, 64:128]
    for b in range(4):
        own = slice(128 * b, 128 * b + 128)
        for a in range(32):
            gwin[4 * a : 4 * a + 4, own] = agf[b % 2, 2 * a + b // 2]
        tile = agt[b % 2, b // 2]
        for i, out in enumerate((gbin, ggain, gbias)):
            out[:, own] = tile[i : i + 1, :]
        gb1[:, own] = tile[3:5, :]
        gb2[:, own] = tile[5:7, :]
    for copy in outs:
        copy.wait()


def body(frames, enc_taps, enc_bias, enc_proj, w_in, b_in, ln_gain, ln_bias, spec_w1, spec_b1, spec_w2, spec_b2, cotangent):
    vmem = pl.BlockSpec(memory_space=pltpu.VMEM)
    hbm = pl.BlockSpec(memory_space=pltpu.HBM)
    anywhere = pl.BlockSpec(memory_space=pl.ANY)
    shape = jax.ShapeDtypeStruct
    dma = pltpu.SemaphoreType.DMA
    operands = (
        frames, enc_taps, enc_bias.reshape(1, -1), enc_proj.T, w_in, b_in.reshape(1, -1), ln_gain.reshape(1, -1),
        ln_bias.reshape(1, -1), spec_w1, spec_b1, spec_w2, spec_b2, cotangent) + tuple(jnp.asarray(t) for t in tables())
    den, agw, agf, agt = pl.pallas_call(
        kernel,
        out_shape=(shape((ROWS, LAT, WIDTH), BF16), shape((2, 32, 2, 8, 128), F32), shape((2, 64, 4, 128), F32), shape((2, 2, 8, 128), F32)),
        in_specs=[hbm] * 20,
        out_specs=(anywhere,) * 4,
        scratch_shapes=[pltpu.VMEM(x.shape, x.dtype) for x in operands] + [
            pltpu.VMEM((FRAMES, 272, 128), F32),
            pltpu.VMEM((NC, FRAMES, 3, 8, 128), BF16),
            pltpu.VMEM((FRAMES, 8, 128), BF16),
            pltpu.VMEM((FRAMES, 8, 128), BF16),
            pltpu.VMEM((NC, FRAMES, 3, 8, 128), BF16),
            pltpu.VMEM((NC, FRAMES, 8, 128), BF16),
            pltpu.VMEM((NC, FRAMES, 8, 128), BF16),
            pltpu.VMEM((FRAMES, 4, 192, 128), F32),
            pltpu.VMEM((512, 144), BF16),
            pltpu.VMEM((32, 512), BF16),
            pltpu.VMEM((16, 32), F32),
            pltpu.VMEM((ROWS, 128, LAT), BF16),
            pltpu.VMEM((ROWS, LAT, WIDTH), F32),
            pltpu.VMEM((ROWS, LAT, WIDTH), F32),
            pltpu.VMEM((ROWS, LAT, 1), F32),
            pltpu.VMEM((ROWS, LAT, WIDTH), BF16),
            pltpu.VMEM((4, 8 * ND, 128), F32),
            pltpu.VMEM((4, ND, 8, 512), BF16),
            pltpu.VMEM((4, ND, 8, 512), BF16),
            pltpu.VMEM((2, 256, 256), BF16),
            pltpu.VMEM((2, 256, 256), BF16),
            pltpu.VMEM((8, WIDTH), F32),
            pltpu.VMEM((32, 8, 128), F32),
            pltpu.VMEM((32, 8, 128), F32),
            pltpu.VMEM((2, 32, 2, 8, 128), F32),
            pltpu.VMEM((2, 64, 4, 128), F32),
            pltpu.VMEM((64, 4, 128), F32),
            pltpu.VMEM((64, 4, 128), F32),
            pltpu.VMEM((64, 4, 128), F32),
            pltpu.VMEM((2, 64, 4, 128), F32),
            pltpu.VMEM((2, 2, 8, 128), F32),
            pltpu.VMEM((2, 8, 128), F32),
            pltpu.VMEM((2, 8, 128), F32),
            pltpu.VMEM((2, 64, 8, 128), F32),
            pltpu.VMEM((2, 2, 8, 128), F32),
            dma((20,)), dma((8,)), dma(()), dma(()), dma((2,)), dma((2,)), dma((4,)), dma((4,)), dma((4,)),
            dma(()), dma(()), dma(()), dma(()), dma(()), dma(()), dma(()), dma(()), dma((5,)), dma((5,)), dma((2,)), dma((2,)), dma((2,)), dma((2,)),
        ],
        compiler_params=pltpu.CompilerParams(
            collective_id=0, has_side_effects=True, vmem_limit_bytes=VMEM_LIMIT),
        name="step",
    )(*(pltpu.with_memory_space_constraint(x, pltpu.HBM) for x in operands))
    den, gwin, gbin, ggain, gbias, gw1, gb1, gw2, gb2 = pl.pallas_call(
        finish,
        out_shape=(
            shape((ROWS, LAT, WIDTH), BF16), shape((128, WIDTH), F32), shape((1, WIDTH), F32), shape((1, WIDTH), F32),
            shape((1, WIDTH), F32), shape((2, 8, 64, 64), F32), shape((2, WIDTH), F32), shape((2, 8, 64, 64), F32),
            shape((2, WIDTH), F32)),
        in_specs=[vmem] * 4,
        out_specs=(hbm,) + (vmem,) * 8,
        scratch_shapes=[dma((ROWS,))],
        compiler_params=pltpu.CompilerParams(vmem_limit_bytes=16 * 1024 * 1024),
        name="finish",
    )(den, agw, agf, agt)
    return (den, gwin, gbin.reshape(-1), ggain.reshape(-1), gbias.reshape(-1), gw1, gb1, gw2, gb2)


def solution(mesh):
    return jax.shard_map(
        body,
        mesh=mesh,
        in_specs=(P(None, "rows", "cols"),) + (P(),) * 11 + (P(("rows", "cols"), None, None),),
        out_specs=(P(("rows", "cols"), None, None),) + (P(),) * 8,
        check_vma=False,
    )
```

```python
import itertools
import math
import random

import jax
import jax.numpy as jnp
import ml_dtypes
import numpy as np
from jax import lax
from jax.experimental import pallas as pl
from jax.experimental.pallas import tpu as pltpu
from jax.sharding import PartitionSpec as P

F32 = jnp.float32
BF16 = jnp.bfloat16
HIGHEST = lax.Precision.HIGHEST

NR, NC = 8, 16
ND = NR * NC
LAT = 512
WIDTH = 512
KH = 128
ROWS = 4
FRAMES = 4


def far_first():
    offsets = [o for o in itertools.product(range(4), range(2), range(2), range(4), range(2)) if any(o)]
    random.Random(1).shuffle(offsets)
    y_hops = {(0, 0): 0, (1, 0): 1, (0, 1): 2, (1, 1): 1}
    return sorted(offsets, key=lambda o: -(min(o[0], 4 - o[0]) + min(o[3], 4 - o[3]) + y_hops[o[1], o[2]]))


PEERS = far_first()
OUT_FIRST = 40
OUT_SECOND = 40
SUMS_AT = 4
VMEM_LIMIT = 44 * 1024 * 1024
EPS = 1e-05
FACTOR = LAT ** (-0.5)
CUBE = 0.044715
ROOT = math.sqrt(2.0 / math.pi)


def tables():
    n = np.arange(LAT)
    k = np.arange(ND)
    angle = ((k[:, None] * n[None, :]) % LAT).astype(np.float32) * np.float32(2.0 * math.pi / LAT)
    fwd = np.stack([np.cos(angle.astype(np.float64)), -np.sin(angle.astype(np.float64))]).astype(np.float32)
    inv = fwd * np.where(k == 0, 1.0, 2.0).astype(np.float32)[None, :, None]
    order = lambda t: t.reshape(2, 32, 4, LAT).transpose(2, 0, 1, 3).reshape(256, LAT).astype(ml_dtypes.bfloat16)
    m = np.arange(KH) - KH // 2
    u = (np.mod(m[:, None] * n[None, :], LAT)).astype(np.float32) * np.float32(2.0 * math.pi / LAT)
    cos, sin = np.cos(u.astype(np.float64)), np.sin(u.astype(np.float64))
    rot = np.concatenate([np.stack([cos, sin], -1), np.stack([-sin, cos], -1)], 0)
    rot = rot.astype(np.float32).reshape(2 * KH, 2 * LAT).astype(ml_dtypes.bfloat16)
    wf, wi = order(fwd), order(inv)
    place = np.zeros((16, 48, 144), np.float32)
    for y in range(4):
        for x in range(4):
            for part in range(3):
                for tap in range(9):
                    place[4 * y + x, 16 * part + tap, 48 * part + 8 * (y + tap // 3) + x + tap % 3] = 1.0
                place[4 * y + x, 16 * part + 9, 48 * part + 6] = 1.0
    return wf, wi, rot, place.astype(ml_dtypes.bfloat16)


def dot(a, b, precision=None):
    return jnp.dot(a, b, preferred_element_type=F32, precision=precision)


def dot_t(a, b, dims, precision=None):
    return lax.dot_general(a, b, (dims, ((), ())), preferred_element_type=F32, precision=precision)


def gelu_pair(v):
    squared = v * v
    t = jnp.tanh(ROOT * (v + CUBE * (squared * v)))
    half = 0.5 * (1.0 + t)
    slope = half + 0.5 * v * (1.0 - t * t) * (ROOT * (1.0 + (3.0 * CUBE) * squared))
    return v * half, slope


def kernel(
    frames_h, taps_h, bias_h, proj_h, w_in_h, b_in_h, gain_h, lbias_h, w1_h, b1_h, w2_h, b2_h, cot_h,
    wf_h, wi_h, rot_h, place_h,
    den_hbm, agw_out, agf_out, agt_out,
    frames, taps, bias, proj, w_in, b_in, gain, lbias, w1, b1, w2, b2, cot, wf, wi, rot, place, wft, wit, rott,
    ft, fsend, htop, hbot, frecv, rtop, rbot, est, wbig, projt, tp, lat, emb, nrm, istd, den,
    stage, snd, rcv, wc1, wc2, bc, wsend, wrecv, agw, fsnd, fpair, fsum, frcv, agf, tiny, tpair, tsum, trcv, agt,
    isem, lsem, fss, frs, hss, hrs, ass, ars, als, wss, wrs, gss, grs, rss, rrs, qss, qrs, pss, prs, tss, trs, uss, urs,
):
    r = lax.axis_index("rows")
    c = lax.axis_index("cols")
    me = r * NC + c
    kg = me // 4
    cg = lax.rem(me, 4)
    core = lax.rem(c, 2)
    chip = me // 2
    partner = me + 1 - 2 * core
    owner = (13 + 24 * core, 50 - 24 * core)

    barrier = pltpu.get_barrier_semaphore()

    @pl.loop(1, NR)
    def _(a):
        row = lax.rem(r + a, NR) * NC
        for k in range(NC):
            pl.semaphore_signal(barrier, inc=1, device_id=row + k, device_id_type=pl.DeviceIdType.LOGICAL)

    for k in range(1, NC):
        pl.semaphore_signal(
            barrier, inc=1, device_id=r * NC + lax.rem(c + k, NC), device_id_type=pl.DeviceIdType.LOGICAL)

    inputs = {}
    for i, (src, dst) in enumerate((
            (frames_h, frames), (cot_h, cot), (wi_h, wi), (taps_h, taps), (bias_h, bias), (place_h, place), (proj_h, proj),
            (w1_h, w1), (w2_h, w2), (b1_h, b1), (b2_h, b2), (w_in_h, w_in), (b_in_h, b_in), (gain_h, gain),
            (lbias_h, lbias), (wf_h, wf), (rot_h, rot))):
        inputs[i] = pltpu.make_async_copy(src, dst, isem.at[i])
        inputs[i].start()

    def arrive(*which):
        for i in which:
            inputs[i].wait()

    at_z = [lax.rem(lax.rem(r, 4) + i, 4) * NC for i in range(4)]
    at_yl = [lax.rem(r // 4 + i, 2) * 4 * NC for i in range(2)]
    at_yh = [lax.rem(c // 8 + i, 2) * 8 for i in range(2)]
    at_x = [lax.rem(lax.rem(c // 2, 4) + i, 4) * 2 for i in range(4)]
    at_core = [core, 1 - core]
    at_row = {(z, yl): at_z[z] + at_yl[yl] for z in range(4) for yl in range(2)}
    at_col = {(yh, x, k): at_yh[yh] + at_x[x] + at_core[k] for yh in range(2) for x in range(4) for k in range(2)}

    def every_peer(act, part=slice(None)):
        for z, yl, yh, x, k in PEERS[part]:
            act(at_row[z, yl] + at_col[yh, x, k])

    def every_chip(act):
        for z, yl, yh, x, k in PEERS:
            if k == 0:
                act(at_row[z, yl] + at_col[yh, x, k])

    def remote(src, dst, ss, rs, d):
        return pltpu.make_async_remote_copy(src, dst, ss, rs, device_id=d, device_id_type=pl.DeviceIdType.LOGICAL)

    def batch(ref, ss, rs):
        return remote(ref, ref, ss, rs, partner)

    zero8 = jnp.zeros((8, 128), F32)
    arrive(0)
    for f in range(FRAMES):
        ft[f, 0:8, :] = zero8
        ft[f, 264:272, :] = zero8
        ft[f, 8:264, :] = frames[f].astype(F32)
    for f in range(FRAMES):
        for j in range(NC):
            fsend[j, f] = ft[f, 16 * j + 7 : 16 * j + 31, :].reshape(3, 8, 128).astype(BF16)
        htop[f] = ft[f, 263:271, :].astype(BF16)
        hbot[f] = ft[f, 7:15, :].astype(BF16)

    def put_rows(h, value):
        for k4 in range(4):
            for p in range(2):
                rows = value[k4 * 64 + p * 32 : k4 * 64 + p * 32 + 32, :]
                for g in range(4):
                    stage[k4, pl.ds(8 * g + 2 * h + p, 32, stride=32), :] = rows[:, 128 * g : 128 * g + 128]

    def pack(e):
        for k4 in range(4):
            snd[e, :, :, 128 * k4 : 128 * k4 + 128] = stage[k4].reshape(ND, 8, 128).astype(BF16)

    def send_own(e):
        pltpu.make_async_copy(snd.at[e, me], rcv.at[e, me], als.at[e]).start()

    def send_all(e, part=slice(None)):
        every_peer(lambda d: remote(snd.at[e, d], rcv.at[e, me], ass.at[e], ars.at[e], d).start(), part)

    def recv_all(e):
        pltpu.make_async_copy(snd.at[e, me], rcv.at[e, me], als.at[e]).wait()
        batch(rcv.at[e, pl.ds(0, ND - 1)], ass.at[e], ars.at[e]).wait_recv()

    pl.semaphore_wait(barrier, ND - 1)

    for j in [at_col[yh, x, k] for z, yl, yh, x, k in PEERS if z == yl == 0]:
        remote(fsend.at[j], frecv.at[c], fss, frs, r * NC + j).start()

    own_frames = pltpu.make_async_copy(fsend.at[c], frecv.at[c], lsem.at[1])
    own_frames.start()

    @pl.when(r < NR - 1)
    def _():
        remote(htop, rtop.at[c], hss.at[0], hrs.at[0], (r + 1) * NC).start()

    @pl.when(r > 0)
    def _():
        remote(hbot, rbot.at[c], hss.at[1], hrs.at[1], r * NC - 1).start()

    has_top = jnp.logical_and(c == 0, r > 0)
    has_bot = jnp.logical_and(c == NC - 1, r < NR - 1)

    @pl.when(jnp.logical_not(has_top))
    def _():
        rtop[...] = jnp.zeros(rtop.shape, BF16)

    @pl.when(jnp.logical_not(has_bot))
    def _():
        rbot[...] = jnp.zeros(rbot.shape, BF16)

    arrive(1, 2)
    for h in range(ROWS):
        put_rows(h, dot(wi[...], cot[h]) * FACTOR)
    pack(0)

    arrive(3, 4, 5, 6, 7, 8, 9, 10)
    tp[...] = jnp.zeros(tp.shape, F32)
    tp[0:9, :] = taps[...]
    tp[9:10, :] = bias[...]
    whole = tp[...]
    high = whole.astype(BF16)
    rest = whole - high.astype(F32)
    mid = rest.astype(BF16)
    low = (rest - mid.astype(F32)).astype(BF16)
    parts = jnp.concatenate([high, mid, low], axis=0)
    for yx in range(16):
        wbig[32 * yx : 32 * yx + 32, :] = dot_t(parts, place[yx], ((0,), (0,))).astype(BF16)
    row = lax.broadcasted_iota(jnp.int32, (512, 512), 0)
    col = lax.broadcasted_iota(jnp.int32, (512, 512), 1)
    to_yxc = (row == (col & 31) * 16 + (col >> 5)).astype(F32).astype(BF16)
    projt[...] = dot(proj[...], to_yxc).astype(BF16)
    to_phase = (row == (col & 127) * 4 + (col >> 7)).astype(F32).astype(BF16)
    for wc, w in ((wc1, w1), (wc2, w2)):
        wc[...] = jnp.zeros(wc.shape, BF16)
        for b in range(2):
            lo, hi = 64 * b, 64 * b + 64
            for p in range(2):
                whole = w[p, 2 * cg + b]
                high = whole.astype(BF16)
                for i, v in enumerate((high, (whole - high.astype(F32)).astype(BF16))):
                    if p == 0:
                        wc[i, lo:hi, lo:hi] = v
                        wc[i, 128 + lo : 128 + hi, 128 + lo : 128 + hi] = v
                    else:
                        wc[i, lo:hi, 128 + lo : 128 + hi] = v
                        wc[i, 128 + lo : 128 + hi, lo:hi] = -v
    lanes = pl.ds(pl.multiple_of(cg * 128, 128), 128)
    bias1 = jnp.concatenate([b1[0:1, lanes], b1[1:2, lanes]], axis=1)
    bias2 = jnp.concatenate([b2[0:1, lanes], b2[1:2, lanes]], axis=1)
    for f in range(FRAMES):
        for t in range(4):
            est[f, t, pl.ds(6, 24, stride=8), :] = jnp.ones((24, 128), F32)
            est[f, t, pl.ds(7, 24, stride=8), :] = jnp.zeros((24, 128), F32)
    eye = (row == col).astype(F32).astype(BF16)
    arrive(15, 16)
    wft[...] = dot_t(wf[...], eye[0:256, 0:256], ((0,), (0,))).astype(BF16)
    wit[...] = dot_t(wi[...], eye[0:256, 0:256], ((0,), (0,))).astype(BF16)
    for i in range(2):
        own = slice(512 * i, 512 * i + 512)
        rott[own, :] = dot_t(rot[:, own], eye[0:256, 0:256], ((0,), (0,))).astype(BF16)

    send_own(0)

    own_frames.wait()
    batch(frecv.at[pl.ds(0, NC - 1)], fss, frs).wait_recv()

    @pl.when(has_top)
    def _():
        batch(rtop, hss.at[0], hrs.at[0]).wait_recv()

    @pl.when(has_bot)
    def _():
        batch(rbot, hss.at[1], hrs.at[1]).wait_recv()

    send_all(0)
    split = []
    for g in range(4):
        pieces = []
        for j in range(4):
            v = frecv[4 * g + j].astype(F32)
            up = v[:, 0] + rtop[4 * g + j].astype(F32)
            down = v[:, 2] + rbot[4 * g + j].astype(F32)
            pieces.append(jnp.stack([up, v[:, 1], down], axis=1).reshape(96, 128).astype(BF16))
        split.append(dot(jnp.concatenate(pieces, axis=1), to_phase))
    lane = lax.broadcasted_iota(jnp.int32, (96, 512), 1)
    first = jnp.concatenate([s[:, 0:128] for s in split], axis=1)
    last = jnp.concatenate([s[:, 384:512] for s in split], axis=1)
    before = jnp.where(lane == 0, 0.0, pltpu.roll(last, 1, axis=1))
    after = jnp.where(lane == LAT - 1, 0.0, pltpu.roll(first, LAT - 1, axis=1))
    for t in range(4):
        own = slice(128 * t, 128 * t + 128)
        planes = [before[:, own]] + [split[t][:, 128 * q : 128 * q + 128] for q in range(4)] + [after[:, own]]
        for x, plane in enumerate(planes):
            for f in range(FRAMES):
                est[f, t, pl.ds(x, 24, stride=8), :] = plane[24 * f : 24 * f + 24, :]

    @pl.loop(0, ROWS)
    def _(h):
        for f in range(FRAMES):
            top = pl.multiple_of(32 * h, 32)
            patch = jnp.concatenate([est[f, t, pl.ds(top, 48), :] for t in range(4)], axis=1).astype(BF16)
            hidden = dot(wbig[...], jnp.concatenate([patch, patch, patch], axis=0))
            hidden = jnp.maximum(hidden, 0.0).astype(BF16)
            lat[h, 32 * f : 32 * f + 32, :] = dot(projt[...], hidden).astype(BF16)

    arrive(11, 12, 13, 14)
    for h in range(ROWS):
        embedded = dot_t(lat[h], w_in[...], ((0,), (0,))) + b_in[...]
        emb[h] = embedded
        centered = embedded - jnp.mean(embedded, axis=1, keepdims=True)
        inverse = lax.rsqrt(jnp.mean(centered * centered, axis=1, keepdims=True) + EPS)
        normalized = centered * inverse
        istd[h] = inverse
        nrm[h] = normalized
        normed = (normalized * gain[...] + lbias[...]).astype(BF16)
        put_rows(h, dot(wf[...], normed) * FACTOR)
    pack(1)
    send_own(1)
    send_all(1)

    def to_modes(e):
        x = rcv[e].reshape(2 * LAT, 512)
        return stacked(dot(rot[...], x) * FACTOR)

    def stacked(v):
        return jnp.concatenate(
            [jnp.concatenate([v[0:KH, 128 * q : 128 * q + 128], v[KH:, 128 * q : 128 * q + 128]], axis=1) for q in range(4)], axis=0)

    def unstacked(v):
        return jnp.concatenate(
            [jnp.concatenate([v[KH * q : KH * q + KH, 128 * p : 128 * p + 128] for q in range(4)], axis=1) for p in range(2)], axis=0)

    def to_back(e, v):
        back = dot(rott[...], unstacked(v).astype(BF16)) * FACTOR
        snd[e] = back.reshape(ND, 8, 512).astype(BF16)

    def dot3(v, wc, side=0):
        high = v.astype(BF16)
        low = (v - high.astype(F32)).astype(BF16)
        dims = ((1,), (side,))
        return dot_t(high, wc[0], dims) + (dot_t(high, wc[1], dims) + dot_t(low, wc[0], dims))

    recv_all(0)
    grad = to_modes(0)
    grad_act = dot3(grad, wc2, 1)
    recv_all(1)
    coeffs = to_modes(1)
    pre = dot3(coeffs, wc1) + bias1
    act, slope = gelu_pair(pre)
    back = grad_act * slope
    to_back(3, dot3(back, wc1, 1))
    send_own(3)
    send_all(3)

    half = lax.broadcasted_iota(jnp.int32, (64, 128), 1) < 64

    def weight_grad(left, right):
        g = dot_t(left, right, ((0,), (0,)), HIGHEST)
        real = g[0:128, 0:128] + g[128:256, 128:256]
        imag = g[0:128, 128:256] - g[128:256, 0:128]
        return [jnp.where(half, v[0:64, :], v[64:128, :]) for v in (real, imag)]

    tiles = weight_grad(coeffs, back) + weight_grad(act, grad)
    wsend[...] = jnp.concatenate(tiles, axis=0).reshape(32, 8, 128)
    wrecv[kg] = wsend[kg]

    @pl.loop(1, 32)
    def _(i):
        j = lax.rem(kg + i, 32)
        remote(wsend.at[j], wrecv.at[kg], wss, wrs, 4 * j + cg).start()

    to_back(2, dot3(act, wc2) + bias2)

    sum1 = jnp.sum(back, axis=0, keepdims=True)
    sum2 = jnp.sum(grad, axis=0, keepdims=True)
    bc[...] = jnp.zeros(bc.shape, F32)
    for p in range(2):
        bc[p : p + 1, lanes] = sum1[:, 128 * p : 128 * p + 128]
        bc[2 + p : 3 + p, lanes] = sum2[:, 128 * p : 128 * p + 128]

    def get_rows(e, h):
        blocks = []
        for k4 in range(4):
            for q in range(2):
                blocks.append(jnp.concatenate(
                    [stage[k4, pl.ds(8 * g + 2 * h + q, 32, stride=32), :] for g in range(4)], axis=1))
        return jnp.concatenate(blocks, axis=0).astype(BF16)

    def unpack(e):
        for k4 in range(4):
            stage[k4] = rcv[e, :, :, 128 * k4 : 128 * k4 + 128].astype(F32).reshape(8 * ND, 128)

    recv_all(3)
    send_own(2)
    send_all(2, slice(0, OUT_FIRST))
    unpack(3)
    mine = agw.at[core, kg, lax.rem(chip, 2)]
    wide = trcv.at[0, pl.ds(0, 63)]

    def send_spectral_sums():
        batch(wrecv.at[pl.ds(0, 31)], wss, wrs).wait_recv()
        agw[core, kg, lax.rem(chip, 2)] = jnp.sum(wrecv[...], axis=0)
        every_chip(lambda d: remote(mine, mine, gss, grs, d).start())

    scaled_gain = gain[...] * FACTOR
    sums = [jnp.zeros((1, WIDTH), F32) for _ in range(3)]
    weight = jnp.zeros((128, WIDTH), F32)
    for h in range(ROWS):
        if SUMS_AT == h:
            send_spectral_sums()
        gn = dot(wft[...], get_rows(3, h))
        normalized = nrm[h]
        sums[1] = sums[1] + jnp.sum(gn * normalized, axis=0, keepdims=True)
        sums[2] = sums[2] + jnp.sum(gn, axis=0, keepdims=True)
        scaled = gn * scaled_gain
        ge = cot[h].astype(F32) + istd[h] * (
            scaled
            - jnp.mean(scaled, axis=1, keepdims=True)
            - normalized * jnp.mean(scaled * normalized, axis=1, keepdims=True))
        sums[0] = sums[0] + jnp.sum(ge, axis=0, keepdims=True)
        weight = weight + dot(lat[h], ge.astype(BF16))
    sums = [sums[0], sums[1] * FACTOR, sums[2] * FACTOR]

    for b in range(4):
        own = slice(128 * b, 128 * b + 128)
        for a in range(32):
            fsnd[b % 2, 2 * a + b // 2] = weight[4 * a : 4 * a + 4, own]
        tiny[b % 2, b // 2] = jnp.concatenate([v[:, own] for v in sums] + [bc[0:4, own], jnp.zeros((1, 128), F32)], axis=0)
    remote(fsnd.at[1 - core], fpair, pss.at[0], prs.at[0], partner).start()
    remote(tiny.at[1 - core], tpair, pss.at[3], prs.at[3], partner).start()
    batch(fpair, pss.at[0], prs.at[0]).wait_recv()
    fsum[...] = fsnd[core] + fpair[...]
    frcv[chip] = fsum[chip]
    every_chip(lambda d: remote(fsum.at[d // 2], frcv.at[chip], rss, rrs, d).start())
    batch(tpair, pss.at[3], prs.at[3]).wait_recv()
    tsum[...] = tiny[core] + tpair[...]
    for t in range(2):
        trcv[t, chip] = tsum[t]

        @pl.when(chip != owner[t])
        def _():
            remote(tsum.at[t], trcv.at[t, chip], tss.at[t], trs.at[t], 2 * owner[t] + core).start()

    send_all(2, slice(OUT_FIRST, OUT_SECOND))
    if SUMS_AT == 4:
        send_spectral_sums()

    batch(frcv.at[pl.ds(0, 63)], rss, rrs).wait_recv()
    agf[core, chip] = jnp.sum(frcv[...], axis=0)
    every_chip(lambda d: remote(agf.at[core, chip], agf.at[core, chip], qss, qrs, d).start())
    for t in range(2):

        @pl.when(chip == owner[t])
        def _():
            batch(trcv.at[t, pl.ds(0, 63)], tss.at[t], trs.at[t]).wait_recv()
            agt[core, t] = jnp.sum(trcv[t], axis=0)
            every_chip(lambda d: remote(agt.at[core, t], agt.at[core, t], uss.at[t], urs.at[t], d).start())

    if SUMS_AT == 5:
        send_spectral_sums()
    send_all(2, slice(OUT_SECOND, None))

    batch(wide, gss, grs).wait_recv()
    remote(agw.at[core], agw.at[core], pss.at[1], prs.at[1], partner).start()
    batch(frcv.at[pl.ds(0, 63)], qss, qrs).wait_recv()
    remote(agf.at[core], agf.at[core], pss.at[2], prs.at[2], partner).start()
    for t in range(2):

        @pl.when(chip != owner[t])
        def _():
            batch(agt.at[core, t], uss.at[t], urs.at[t]).wait_recv()

    remote(agt.at[core], agt.at[core], pss.at[4], prs.at[4], partner).start()
    recv_all(2)
    unpack(2)
    for h in range(ROWS):
        den[h] = (emb[h] + dot(wit[...], get_rows(2, h)) * FACTOR).astype(BF16)
        pltpu.make_async_copy(den.at[h], den_hbm.at[h], lsem.at[2 + h]).start()

    batch(agw.at[0], pss.at[1], prs.at[1]).wait_recv()
    agw_copy = pltpu.make_async_copy(agw, agw_out, lsem.at[6])
    agw_copy.start()
    batch(agf.at[0], pss.at[2], prs.at[2]).wait_recv()
    agf_copy = pltpu.make_async_copy(agf, agf_out, lsem.at[7])
    agf_copy.start()
    batch(agt.at[0], pss.at[4], prs.at[4]).wait_recv()
    agt_copy = pltpu.make_async_copy(agt, agt_out, lsem.at[0])
    agt_copy.start()

    agw_copy.wait()
    agf_copy.wait()
    agt_copy.wait()
    for h in range(ROWS):
        pltpu.make_async_copy(den.at[h], den_hbm.at[h], lsem.at[2 + h]).wait()
    batch(frecv.at[pl.ds(0, NC - 1)], fss, frs).wait_send()

    @pl.when(r < NR - 1)
    def _():
        batch(htop, hss.at[0], hrs.at[0]).wait_send()

    @pl.when(r > 0)
    def _():
        batch(hbot, hss.at[1], hrs.at[1]).wait_send()

    for e in range(4):
        batch(rcv.at[e, pl.ds(0, ND - 1)], ass.at[e], ars.at[e]).wait_send()
    batch(wrecv.at[pl.ds(0, 31)], wss, wrs).wait_send()
    batch(fpair, pss.at[0], prs.at[0]).wait_send()
    batch(agw.at[0], pss.at[1], prs.at[1]).wait_send()
    batch(agf.at[0], pss.at[2], prs.at[2]).wait_send()
    batch(tpair, pss.at[3], prs.at[3]).wait_send()
    batch(agt.at[0], pss.at[4], prs.at[4]).wait_send()
    batch(wide, gss, grs).wait_send()
    batch(frcv.at[pl.ds(0, 63)], rss, rrs).wait_send()
    batch(frcv.at[pl.ds(0, 63)], qss, qrs).wait_send()
    for t in range(2):

        @pl.when(chip != owner[t])
        def _():
            batch(tsum.at[t], tss.at[t], trs.at[t]).wait_send()

        @pl.when(chip == owner[t])
        def _():
            batch(trcv.at[t, pl.ds(0, 63)], uss.at[t], urs.at[t]).wait_send()


def finish(den_in, agw, agf, agt, den_out, gwin, gbin, ggain, gbias, gw1, gb1, gw2, gb2, sem):
    outs = [pltpu.make_async_copy(den_in.at[h], den_out.at[h], sem.at[h]) for h in range(ROWS)]
    for copy in outs:
        copy.start()
    for w, gw in enumerate((gw1, gw2)):
        for p in range(2):
            for g in range(4):
                v = agw[g % 2, 16 * w + 8 * p : 16 * w + 8 * p + 8, g // 2].reshape(64, 128)
                gw[p, 2 * g] = v[:, 0:64]
                gw[p, 2 * g + 1] = v[:, 64:128]
    for b in range(4):
        own = slice(128 * b, 128 * b + 128)
        for a in range(32):
            gwin[4 * a : 4 * a + 4, own] = agf[b % 2, 2 * a + b // 2]
        tile = agt[b % 2, b // 2]
        for i, out in enumerate((gbin, ggain, gbias)):
            out[:, own] = tile[i : i + 1, :]
        gb1[:, own] = tile[3:5, :]
        gb2[:, own] = tile[5:7, :]
    for copy in outs:
        copy.wait()


def body(frames, enc_taps, enc_bias, enc_proj, w_in, b_in, ln_gain, ln_bias, spec_w1, spec_b1, spec_w2, spec_b2, cotangent):
    vmem = pl.BlockSpec(memory_space=pltpu.VMEM)
    hbm = pl.BlockSpec(memory_space=pltpu.HBM)
    anywhere = pl.BlockSpec(memory_space=pl.ANY)
    shape = jax.ShapeDtypeStruct
    dma = pltpu.SemaphoreType.DMA
    operands = (
        frames, enc_taps, enc_bias.reshape(1, -1), enc_proj.T, w_in, b_in.reshape(1, -1), ln_gain.reshape(1, -1),
        ln_bias.reshape(1, -1), spec_w1, spec_b1, spec_w2, spec_b2, cotangent) + tuple(jnp.asarray(t) for t in tables())
    den, agw, agf, agt = pl.pallas_call(
        kernel,
        out_shape=(shape((ROWS, LAT, WIDTH), BF16), shape((2, 32, 2, 8, 128), F32), shape((2, 64, 4, 128), F32), shape((2, 2, 8, 128), F32)),
        in_specs=[hbm] * 17,
        out_specs=(anywhere,) * 4,
        scratch_shapes=[pltpu.VMEM(x.shape, x.dtype) for x in operands] + [
            pltpu.VMEM((LAT, 256), BF16),
            pltpu.VMEM((LAT, 256), BF16),
            pltpu.VMEM((2 * LAT, 2 * KH), BF16),
            pltpu.VMEM((FRAMES, 272, 128), F32),
            pltpu.VMEM((NC, FRAMES, 3, 8, 128), BF16),
            pltpu.VMEM((FRAMES, 8, 128), BF16),
            pltpu.VMEM((FRAMES, 8, 128), BF16),
            pltpu.VMEM((NC, FRAMES, 3, 8, 128), BF16),
            pltpu.VMEM((NC, FRAMES, 8, 128), BF16),
            pltpu.VMEM((NC, FRAMES, 8, 128), BF16),
            pltpu.VMEM((FRAMES, 4, 192, 128), F32),
            pltpu.VMEM((512, 144), BF16),
            pltpu.VMEM((32, 512), BF16),
            pltpu.VMEM((16, 32), F32),
            pltpu.VMEM((ROWS, 128, LAT), BF16),
            pltpu.VMEM((ROWS, LAT, WIDTH), F32),
            pltpu.VMEM((ROWS, LAT, WIDTH), F32),
            pltpu.VMEM((ROWS, LAT, 1), F32),
            pltpu.VMEM((ROWS, LAT, WIDTH), BF16),
            pltpu.VMEM((4, 8 * ND, 128), F32),
            pltpu.VMEM((4, ND, 8, 512), BF16),
            pltpu.VMEM((4, ND, 8, 512), BF16),
            pltpu.VMEM((2, 256, 256), BF16),
            pltpu.VMEM((2, 256, 256), BF16),
            pltpu.VMEM((8, WIDTH), F32),
            pltpu.VMEM((32, 8, 128), F32),
            pltpu.VMEM((32, 8, 128), F32),
            pltpu.VMEM((2, 32, 2, 8, 128), F32),
            pltpu.VMEM((2, 64, 4, 128), F32),
            pltpu.VMEM((64, 4, 128), F32),
            pltpu.VMEM((64, 4, 128), F32),
            pltpu.VMEM((64, 4, 128), F32),
            pltpu.VMEM((2, 64, 4, 128), F32),
            pltpu.VMEM((2, 2, 8, 128), F32),
            pltpu.VMEM((2, 8, 128), F32),
            pltpu.VMEM((2, 8, 128), F32),
            pltpu.VMEM((2, 64, 8, 128), F32),
            pltpu.VMEM((2, 2, 8, 128), F32),
            dma((17,)), dma((8,)), dma(()), dma(()), dma((2,)), dma((2,)), dma((4,)), dma((4,)), dma((4,)),
            dma(()), dma(()), dma(()), dma(()), dma(()), dma(()), dma(()), dma(()), dma((5,)), dma((5,)), dma((2,)), dma((2,)), dma((2,)), dma((2,)),
        ],
        compiler_params=pltpu.CompilerParams(
            collective_id=0, has_side_effects=True, vmem_limit_bytes=VMEM_LIMIT),
        name="step",
    )(*(pltpu.with_memory_space_constraint(x, pltpu.HBM) for x in operands))
    den, gwin, gbin, ggain, gbias, gw1, gb1, gw2, gb2 = pl.pallas_call(
        finish,
        out_shape=(
            shape((ROWS, LAT, WIDTH), BF16), shape((128, WIDTH), F32), shape((1, WIDTH), F32), shape((1, WIDTH), F32),
            shape((1, WIDTH), F32), shape((2, 8, 64, 64), F32), shape((2, WIDTH), F32), shape((2, 8, 64, 64), F32),
            shape((2, WIDTH), F32)),
        in_specs=[vmem] * 4,
        out_specs=(hbm,) + (vmem,) * 8,
        scratch_shapes=[dma((ROWS,))],
        compiler_params=pltpu.CompilerParams(vmem_limit_bytes=16 * 1024 * 1024),
        name="finish",
    )(den, agw, agf, agt)
    return (den, gwin, gbin.reshape(-1), ggain.reshape(-1), gbias.reshape(-1), gw1, gb1, gw2, gb2)


def solution(mesh):
    return jax.shard_map(
        body,
        mesh=mesh,
        in_specs=(P(None, "rows", "cols"),) + (P(),) * 11 + (P(("rows", "cols"), None, None),),
        out_specs=(P(("rows", "cols"), None, None),) + (P(),) * 8,
        check_vma=False,
    )
```
